512 devices in a mesh: seq: 64 (over y, z), req: 8 (over x, core).
Axes of the slice: x: 4, y: 4, z: 16, core: 2. Of those that a mesh axis runs over, the one named last changes fastest.
Arguments:
- new_token_queries: bfloat16 [4, 64, 2048], P(None, 'req'), may hold values from -48 to 48
- new_token_keys: bfloat16 [4, 64, 1024], P(None, 'req'), may hold values from -48 to 48
- new_token_values: bfloat16 [4, 64, 1024], P(None, 'req'), may hold values from -6 to 6
- key_cache: bfloat16 [64, 2048, 1024], P('req', 'seq'), may hold values from -48 to 48
- value_cache: bfloat16 [64, 2048, 1024], P('req', 'seq'), may hold values from -6 to 6
- cache_len: int32 [64], P('req'), may hold values from 1 to 2048, 34816 in all
- resid: bfloat16 [4, 64, 2048], P(None, 'req'), may hold values from -6 to 6
- gain: bfloat16 [2048], replicated, may hold values from 0.5 to 1.5
- w_gate: bfloat16 [2048, 6144], P('seq', 'req'), may hold values from -0.125 to 0.125
- w_up: bfloat16 [2048, 6144], P('seq', 'req'), may hold values from -0.125 to 0.125
- w_down: bfloat16 [6144, 2048], P('req', 'seq'), may hold values from -0.078125 to 0.078125
Outputs:
- out: bfloat16 [4, 64, 2048], P(None, 'req')
The draws below stay inside these ranges and needn't reach their ends.
All inputs are finite; a program needn't handle non-finite values. No bound on the sum of `cache_len` on one device may be relied on, other than what follows from the above.
Results may differ from the reference program's by a relative error of at most 0.006.
Values may be sent and summed in bfloat16 or wider, within the bound.
A program may use at most 128 MiB of HBM per device.

```python
import math
import jax
import jax.numpy as jnp
import numpy as np
from jax import lax

D = 2048
QUERY_HEADS = 16
KEY_VALUE_HEADS = 8
HEAD_SIZE = 128
FF = 6144
PAGE_POSITIONS = 32
DECODE_STEPS = 4
REQUEST_COUNT = 64
REQUEST_LENGTH = 2048


def draw_new_token_queries(key, part):
    head_cluster = QUERY_HEADS // KEY_VALUE_HEADS
    sampled_token = jnp.clip(jax.random.normal(jax.random.fold_in(key, 1), (DECODE_STEPS, REQUEST_COUNT, KEY_VALUE_HEADS, head_cluster, HEAD_SIZE), jnp.float32), -6.0, 6.0)
    return sampled_token.reshape(DECODE_STEPS, REQUEST_COUNT, KEY_VALUE_HEADS * head_cluster * HEAD_SIZE).astype(jnp.bfloat16)


def draw_key_cache(key, part):
    sampled_token = jnp.clip(jax.random.normal(jax.random.fold_in(key, 2), (REQUEST_COUNT, REQUEST_LENGTH, KEY_VALUE_HEADS, HEAD_SIZE), jnp.float32), -6.0, 6.0)
    return sampled_token.reshape(REQUEST_COUNT, REQUEST_LENGTH, KEY_VALUE_HEADS * HEAD_SIZE).astype(jnp.bfloat16)


def draw_new_token_keys(key, part):
    sampled_token = jnp.clip(jax.random.normal(jax.random.fold_in(key, 3), (DECODE_STEPS, REQUEST_COUNT, KEY_VALUE_HEADS, HEAD_SIZE), jnp.float32), -6.0, 6.0)
    return sampled_token.reshape(DECODE_STEPS, REQUEST_COUNT, KEY_VALUE_HEADS * HEAD_SIZE).astype(jnp.bfloat16)


def steps_of(rng, shape, pieces, smallest, top_value):
    level = 1.0
    for axis_at, parts in pieces:
        steps = jax.random.uniform(jax.random.fold_in(jax.random.fold_in(rng, 6), axis_at), (parts,), jnp.float32, smallest / len(pieces), top_value / len(pieces))
        level = level * jnp.repeat(jnp.exp(steps), shape[axis_at] // parts).reshape((-1,) + (1,) * (len(shape) - 1 - axis_at))
    return level


def split_up(amount, total, limit, lean):
    weights = [(1 << 20) // math.isqrt(grade ** lean) + 1 for grade in range(2, amount + 1)]
    spare, given = total - limit - (amount - 1), [1] * (amount - 1)
    while spare > 0:
        candidates = [i for i in range(amount - 1) if given[i] < limit]
        whole, budget = sum([weights[i] for i in candidates]), spare
        for i in candidates:
            more = min(limit - given[i], max(1, budget * weights[i] // whole), spare)
            given[i] = given[i] + more
            spare = spare - more
    return np.array([limit] + given)


def uneven(key, amount, total, bound, slope):
    if amount == 2:
        one = jax.random.randint(key, (), max(1, total - bound), min(bound, total - 1) + 1)
        return jnp.stack([one, total - one])
    tallies = jnp.asarray(split_up(amount, total, bound, slope), jnp.int32)
    pairs = (amount - 1) // 2
    donor, sink = tallies[1:1 + 2 * pairs:2], tallies[2:2 + 2 * pairs:2]
    margin = jnp.minimum(donor - 1, bound - sink)
    passed = jax.random.randint(jax.random.fold_in(key, 1), (pairs,), 0, 1 << 20) % (margin + 1)
    tallies = tallies.at[1:1 + 2 * pairs:2].set(donor - passed).at[2:2 + 2 * pairs:2].set(sink + passed)
    return tallies[jax.random.permutation(jax.random.fold_in(key, 2), amount)]


def normal_values(own_key, extent, spread, most, cuts=(), kind=jnp.bfloat16):
    values = jax.random.normal(own_key, extent, jnp.float32) * spread
    if len(cuts) > 0:
        values = steps_of(own_key, extent, cuts, -0.22, 0.18) * values
    return jnp.clip(values, min=-most, max=most).astype(kind)


def setup_inputs(seed: int = 0) -> dict:
    key_list = jax.random.split(jax.random.key(seed), 12)
    new_token_queries = draw_new_token_queries(jax.random.fold_in(key_list[11], 71), 0)
    new_token_keys = draw_new_token_keys(jax.random.fold_in(key_list[11], 71), 0)
    new_token_values = normal_values(key_list[2], (DECODE_STEPS, REQUEST_COUNT, KEY_VALUE_HEADS * HEAD_SIZE), 1.0, 6.0, ((1, 8),))
    key_cache = draw_key_cache(jax.random.fold_in(key_list[11], 71), 0)
    value_cache = normal_values(key_list[4], (REQUEST_COUNT, REQUEST_LENGTH, KEY_VALUE_HEADS * HEAD_SIZE), 1.0, 6.0, ((0, 8), (1, 64)))
    cache_len = uneven(key_list[5], REQUEST_COUNT, REQUEST_COUNT * REQUEST_LENGTH // 4 + REQUEST_LENGTH, REQUEST_LENGTH, 2).astype(jnp.int32)
    resid = normal_values(key_list[6], (DECODE_STEPS, REQUEST_COUNT, D), 1.0, 6.0, ((1, 8),))
    gain = jnp.clip(1.0 + 0.1 * jax.random.normal(key_list[7], (D,), jnp.float32), 0.5, 1.5).astype(jnp.bfloat16)
    w_gate = normal_values(key_list[8], (D, FF), D ** -0.5, 0.125, ((0, 64), (1, 8)))
    w_up = normal_values(key_list[9], (D, FF), D ** -0.5, 0.125, ((0, 64), (1, 8)))
    w_down = normal_values(key_list[10], (FF, D), FF ** -0.5, 0.078125, ((0, 8), (1, 64)))
    return dict(new_token_queries=new_token_queries, new_token_keys=new_token_keys, new_token_values=new_token_values, key_cache=key_cache, value_cache=value_cache, cache_len=cache_len, resid=resid, gain=gain, w_gate=w_gate, w_up=w_up, w_down=w_down)


NEG_FILL = -1e+30
EPSILON = 1e-06

def request_partial(query_vector, key_page_block, value_page_block, length):
    count_of_pages = REQUEST_LENGTH // PAGE_POSITIONS
    key_page_table = key_page_block.astype(jnp.float32).reshape(count_of_pages, PAGE_POSITIONS, KEY_VALUE_HEADS, HEAD_SIZE)
    value_page_table = value_page_block.astype(jnp.float32).reshape(count_of_pages, PAGE_POSITIONS, KEY_VALUE_HEADS, HEAD_SIZE)
    positions = jnp.arange(REQUEST_LENGTH, dtype=jnp.int32).reshape(count_of_pages, PAGE_POSITIONS)
    inside = (positions < length)[None, None]
    scores = jnp.einsum('kgd,pbkd->kgpb', query_vector, key_page_table) / math.sqrt(HEAD_SIZE)
    scores = jnp.where(inside, scores, NEG_FILL)
    highest = lax.optimization_barrier(jnp.max(scores, axis=-1))
    weights = jnp.where(inside, jnp.exp(scores - highest[..., None]), 0.0)
    weights = lax.optimization_barrier(weights.astype(jnp.bfloat16)).astype(jnp.float32)
    totals = lax.optimization_barrier(jnp.sum(weights, axis=-1))
    weighted = jnp.einsum('kgpb,pbkd->kgpd', weights, value_page_table)
    best = lax.optimization_barrier(jnp.max(highest, axis=-1))
    factor = jnp.exp(highest - best[..., None])
    return (best, lax.optimization_barrier(jnp.sum(factor * totals, axis=-1)), jnp.einsum('kgp,kgpd->kgd', factor, weighted))

def reference(new_token_queries, new_token_keys, new_token_values, key_cache, value_cache, cache_len, resid, gain, w_gate, w_up, w_down):
    head_cluster = QUERY_HEADS // KEY_VALUE_HEADS
    results = []
    for decode_step_index in range(DECODE_STEPS):
        query_vector = new_token_queries[decode_step_index].astype(jnp.float32).reshape(REQUEST_COUNT, KEY_VALUE_HEADS, head_cluster, HEAD_SIZE)
        best, totals, weighted = lax.map(lambda packed: request_partial(packed[0], packed[1], packed[2], packed[3]), (query_vector, key_cache, value_cache, cache_len))
        incoming_keys = new_token_keys[:decode_step_index + 1].astype(jnp.float32).reshape(decode_step_index + 1, REQUEST_COUNT, KEY_VALUE_HEADS, HEAD_SIZE)
        incoming_values = new_token_values[:decode_step_index + 1].astype(jnp.float32).reshape(decode_step_index + 1, REQUEST_COUNT, KEY_VALUE_HEADS, HEAD_SIZE)
        fresh_scores = jnp.einsum('rkgd,trkd->rkgt', query_vector, incoming_keys) / math.sqrt(HEAD_SIZE)
        fresh_max = lax.optimization_barrier(jnp.max(fresh_scores, axis=-1))
        fresh_weights = jnp.exp(fresh_scores - fresh_max[..., None])
        fresh_weights = lax.optimization_barrier(fresh_weights.astype(jnp.bfloat16)).astype(jnp.float32)
        fresh_total = lax.optimization_barrier(jnp.sum(fresh_weights, axis=-1))
        fresh_acc = jnp.einsum('rkgt,trkd->rkgd', fresh_weights, incoming_values)
        peak = jnp.maximum(best, fresh_max)
        former = jnp.exp(best - peak)
        latter = jnp.exp(fresh_max - peak)
        numerator = former[..., None] * weighted + latter[..., None] * fresh_acc
        denominator = former * totals + latter * fresh_total
        attention = (numerator / denominator[..., None]).reshape(REQUEST_COUNT, D).astype(jnp.bfloat16)
        attention = lax.optimization_barrier(attention).astype(jnp.float32)
        stream = (resid[decode_step_index].astype(jnp.float32) + attention).astype(jnp.bfloat16)
        stream = lax.optimization_barrier(stream).astype(jnp.float32)
        scaled = lax.rsqrt(lax.optimization_barrier(jnp.mean(stream * stream, axis=-1, keepdims=True)) + EPSILON)
        normed = (stream * scaled * gain.astype(jnp.float32)).astype(jnp.bfloat16)
        gate_sum = jnp.dot(normed, w_gate, preferred_element_type=jnp.float32)
        up_sum = jnp.dot(normed, w_up, preferred_element_type=jnp.float32)
        hidden = (jax.nn.silu(gate_sum) * up_sum).astype(jnp.bfloat16)
        down_sum = jnp.dot(hidden, w_down, preferred_element_type=jnp.float32)
        results.append((stream + down_sum).astype(jnp.bfloat16))
    return jnp.stack(results)
```

```python
import math

import jax
import jax.numpy as jnp
from jax import lax
from jax.sharding import PartitionSpec as P

QUERY_HEADS = 16
KEY_VALUE_HEADS = 8
HEAD_SIZE = 128
NEG_FILL = -1e30
EPSILON = 1e-06


def partial_softmax(q, keys, values, valid):
    scores = jnp.einsum("rkmd,rbkd->rkmb", q, keys, preferred_element_type=jnp.float32) / math.sqrt(HEAD_SIZE)
    inside = valid[:, None]
    scores = jnp.where(inside, scores, NEG_FILL)
    highest = jnp.max(scores, axis=-1)
    weights = jnp.where(inside, jnp.exp(scores - highest[..., None]), 0.0).astype(jnp.bfloat16)
    totals = jnp.sum(weights.astype(jnp.float32), axis=-1)
    weighted = jnp.einsum("rkmb,rbkd->rkmd", weights, values, preferred_element_type=jnp.float32)
    return highest, totals, weighted


def body(q, nk, nv, kc, vc, cache_len, resid, gain, w_gate, w_up, w_down):
    steps, rows, model = q.shape
    page = kc.shape[1]
    width = w_gate.shape[0]
    units = w_gate.shape[1]
    group = QUERY_HEADS // KEY_VALUE_HEADS
    me = lax.axis_index("seq")
    positions = me * page + jnp.arange(page, dtype=jnp.int32)
    valid = (positions[None, :] < cache_len[:, None])[:, None, :]
    qv = q.reshape(steps, rows, KEY_VALUE_HEADS, group, HEAD_SIZE).transpose(1, 2, 0, 3, 4)
    qv = qv.reshape(rows, KEY_VALUE_HEADS, steps * group, HEAD_SIZE)
    keys = kc.reshape(rows, page, KEY_VALUE_HEADS, HEAD_SIZE)
    values = vc.reshape(rows, page, KEY_VALUE_HEADS, HEAD_SIZE)
    local = partial_softmax(qv, keys, values, jnp.broadcast_to(valid, (rows, steps * group, page)))
    highest = lax.pmax(local[0], "seq")
    factor = jnp.exp(local[0] - highest)
    totals, weighted = lax.psum((factor * local[1], factor[..., None] * local[2]), "seq")
    fk = jnp.swapaxes(nk, 0, 1).reshape(rows, steps, KEY_VALUE_HEADS, HEAD_SIZE)
    fv = jnp.swapaxes(nv, 0, 1).reshape(rows, steps, KEY_VALUE_HEADS, HEAD_SIZE)
    step_of = jnp.arange(steps * group, dtype=jnp.int32) // group
    causal = jnp.arange(steps, dtype=jnp.int32)[None, :] <= step_of[:, None]
    fresh = partial_softmax(qv, fk, fv, jnp.broadcast_to(causal[None], (rows, steps * group, steps)))
    peak = jnp.maximum(highest, fresh[0])
    a = jnp.exp(highest - peak)
    b = jnp.exp(fresh[0] - peak)
    total = a * totals + b * fresh[1]
    acc = a[..., None] * weighted + b[..., None] * fresh[2]
    attn = (acc / total[..., None]).astype(jnp.bfloat16)
    attn = attn.reshape(rows, KEY_VALUE_HEADS, steps, group, HEAD_SIZE).transpose(2, 0, 1, 3, 4)
    attn = attn.reshape(steps, rows, model)
    attn = lax.optimization_barrier(attn).astype(jnp.float32)
    stream = (resid.astype(jnp.float32) + attn).astype(jnp.bfloat16)
    stream = lax.optimization_barrier(stream).astype(jnp.float32)
    scaled = lax.rsqrt(jnp.mean(stream * stream, axis=-1, keepdims=True) + EPSILON)
    normed = (stream * scaled * gain.astype(jnp.float32)).astype(jnp.bfloat16)
    own = lax.dynamic_slice_in_dim(normed, me * width, width, 2)
    every = lax.all_gather(own, "req", axis=1, tiled=True).reshape(-1, width)
    joined = jnp.concatenate([w_gate, w_up], axis=1)
    sums = lax.psum(jnp.dot(every, joined, preferred_element_type=jnp.float32), "seq")
    hidden = (jax.nn.silu(sums[:, :units]) * sums[:, units:]).astype(jnp.bfloat16)
    down = jnp.dot(hidden, w_down, preferred_element_type=jnp.float32)
    down = lax.psum_scatter(down.reshape(steps, -1, width), "req", scatter_dimension=1, tiled=True)
    piece = (lax.dynamic_slice_in_dim(stream, me * width, width, 2) + down).astype(jnp.bfloat16)
    return lax.all_gather(piece, "seq", axis=2, tiled=True)


def solution(mesh):
    placed = (
        P(None, "req", None),
        P(None, "req", None),
        P(None, "req", None),
        P("req", "seq", None),
        P("req", "seq", None),
        P("req"),
        P(None, "req", None),
        P(),
        P("seq", "req"),
        P("seq", "req"),
        P("req", "seq"),
    )
    return jax.shard_map(body, mesh=mesh, in_specs=placed, out_specs=P(None, "req", None), check_vma=False)
```

```python
import functools
import math

import jax
import jax.numpy as jnp
from jax import lax
from jax.experimental import pallas as pl
from jax.experimental.pallas import tpu as pltpu
from jax.sharding import PartitionSpec as P

NEG_FILL = -1e30
EPSILON = 1e-06
F32 = jnp.float32
BF16 = jnp.bfloat16
NT = (((1,), (1,)), ((), ()))
SCALE = 1.0 / math.sqrt(128)


def split3(x):
    hi = x.astype(BF16).astype(F32)
    rest = x - hi
    mid = rest.astype(BF16).astype(F32)
    low = (rest - mid).astype(BF16).astype(F32)
    return (hi + pltpu.roll(mid, 16, 1) + pltpu.roll(low, 32, 1)).astype(BF16)


def join3(x):
    return x + pltpu.roll(x, 112, 1) + pltpu.roll(x, 96, 1)


def kernel(
    q_h, nk_h, nv_h, k_h, v_h, len_s, resid_h, gain_h, wg_h, wu_h, wd_h,
    out,
    q_v, nk_v, nv_v, k_v, v_v, res_v, gain_v, wg_v, wu_v, wd_v,
    ws, wr, pa, ra, pb, rb, x_v, pp, rp, hh, dd, rd, ee, re,
    lsem,
    ws_s, ws_r, a_s, a_r, b_s, b_r, c_s, c_r, d_s, d_r, e_s, e_r,
    f_s, f_r, g_s, g_r, h_s, h_r, i_s, i_r, j_s, j_r,
):
    s = lax.axis_index("seq")
    q = lax.axis_index("req")
    y = lax.div(s, 16)
    z = lax.rem(s, 16)
    kb = lax.rem(z, 2)
    tg = lax.div(z, 2)
    t = lax.div(z, 4)
    g = lax.rem(tg, 2)
    k = y * 2 + kb
    head = k * 2 + g
    zpair = z + 1 - 2 * kb
    zhi = lax.div(z, 8)
    zlo = lax.rem(z, 8)

    def at(yy, zz):
        return yy * 16 + zz

    y_peers = [(at(lax.rem(y + d, 4), z), q) for d in range(1, 4)]
    z_peers = [(at(y, lax.rem(z + d, 16)), q) for d in range(1, 16)]
    q_peers = [(s, lax.rem(q + d, 8)) for d in range(1, 8)]
    diag_peers = [(at(lax.rem(y + d, 4), zpair), q) for d in range(1, 4)]

    barrier = pltpu.get_barrier_semaphore()
    for peer in y_peers + z_peers + q_peers + diag_peers:
        pl.semaphore_signal(barrier, inc=1, device_id=peer, device_id_type=pl.DeviceIdType.MESH)

    hcol = pl.ds(pl.multiple_of(head * 128, 128), 128)
    kcol = pl.ds(pl.multiple_of(k * 128, 128), 128)
    fcol = pl.ds(pl.multiple_of(k * 256, 256), 256)
    gcol = pl.ds(pl.multiple_of(g * 128, 128), 128)
    loads = [
        (wg_h, wg_v), (wu_h, wu_v), (wd_h, wd_v), (q_h, q_v), (k_h, k_v), (v_h, v_v),
        (nk_h.at[:, :, kcol], nk_v), (nv_h.at[:, :, kcol], nv_v),
        (resid_h.at[t, :, hcol], res_v), (gain_h.at[:, fcol], gain_v),
    ]
    loads = [pltpu.make_async_copy(a, b, lsem.at[i]) for i, (a, b) in enumerate(loads)]
    for c in loads:
        c.start()

    def remote(src, dst, ssem, rsem, peer):
        return pltpu.make_async_remote_copy(
            src_ref=src, dst_ref=dst, send_sem=ssem, recv_sem=rsem,
            device_id=peer, device_id_type=pl.DeviceIdType.MESH,
        )

    sent = []

    def send(copies):
        for c in copies:
            c.start()
        sent.extend(copies)

    for c in loads[:3]:
        c.wait()
    eye = (lax.broadcasted_iota(jnp.int32, (32, 32), 0) == lax.broadcasted_iota(jnp.int32, (32, 32), 1))
    wdt = lax.dot_general(eye.astype(F32).astype(BF16), wd_v[...], NT, preferred_element_type=F32)
    whole = [wg_v[...].astype(F32), wu_v[...].astype(F32), wdt]
    keep = lax.broadcasted_iota(jnp.int32, (32, 128), 1) < 96
    for j in range(8):
        base, off = (96 * j) // 128 * 128, (96 * j) % 128
        for i, w in enumerate(whole):
            if off + 96 <= 128:
                piece = w[:, base:base + 128]
                if off:
                    piece = pltpu.roll(piece, 128 - off, 1)
            else:
                piece = pltpu.roll(w[:, base:base + 256], 256 - off, 1)[:, :128]
            ws[j, :, 128 * i:128 * i + 128] = jnp.where(keep, piece, 0.0).astype(BF16)

    pl.semaphore_wait(barrier, 28)

    for j in range(8):
        zt = 2 * j + zhi
        copy = remote(ws.at[j], wr.at[zlo], ws_s.at[j], ws_r.at[zlo], (at(y, zt), q))

        @pl.when(zt != z)
        def _():
            copy.start()

        @pl.when(zt == z)
        def _():
            wr[zlo] = ws[j]

    for c in loads[3:6]:
        c.wait()
    row = lax.broadcasted_iota(jnp.int32, (64, 256), 0) & 7
    col = lax.broadcasted_iota(jnp.int32, (64, 256), 1)
    limit = jnp.zeros((64, 256), jnp.int32)
    for r in range(8):
        limit = jnp.where(row == r, len_s[r], limit)
    mask = (lax.shift_right_logical(col, 5) == row) & ((col & 31) + s * 32 < limit)
    lane = lax.broadcasted_iota(jnp.int32, (8, 128), 1)
    for yt in range(4):
        tile = jnp.zeros((8, 128), F32)
        for kk in range(2):
            kv = 2 * yt + kk
            qk = jnp.concatenate(
                [
                    q_v[tt, :, 128 * (2 * kv + gg):128 * (2 * kv + gg) + 128].astype(F32)
                    for tt in range(4) for gg in range(2)
                ],
                axis=0,
            ).astype(BF16)
            keys = k_v[:, :, 128 * kv:128 * kv + 128].reshape(256, 128)
            vals = v_v[:, :, 128 * kv:128 * kv + 128].reshape(256, 128)
            sc = lax.dot_general(qk, keys, NT, preferred_element_type=F32) * SCALE
            sc = jnp.where(mask, sc, NEG_FILL)
            top = jnp.max(sc, axis=1, keepdims=True)
            w = jnp.where(mask, jnp.exp(sc - top), 0.0).astype(BF16)
            tot = jnp.sum(w.astype(F32), axis=1, keepdims=True)
            acc = jnp.dot(w, vals, preferred_element_type=F32).astype(BF16)
            pa[yt, 8 * kk:8 * kk + 8] = acc.reshape(8, 8, 128)
            for i in range(8):
                tile = jnp.where(lane == 8 * kk + i, top[8 * i:8 * i + 8], tile)
                tile = jnp.where(lane == 48 + 8 * kk + i, tot[8 * i:8 * i + 8], tile)
        pa[yt, 16] = split3(tile)

    ca = []
    for d in range(1, 4):
        yt = lax.rem(y + d, 4)
        ca.append(remote(pa.at[yt], ra.at[d], a_s.at[d], a_r.at[d], (at(yt, z), q)))
    send(ca)

    for c in loads[6:]:
        c.wait()
    qf = q_v[t, :, hcol]
    nk = nk_v[...].astype(F32).reshape(32, 128).astype(BF16)
    nv = nv_v[...].astype(F32).reshape(32, 128).astype(BF16)
    fs = lax.dot_general(qf, nk, NT, preferred_element_type=F32) * SCALE
    frow = lax.broadcasted_iota(jnp.int32, (8, 32), 0)
    fcl = lax.broadcasted_iota(jnp.int32, (8, 32), 1)
    fmask = ((fcl & 7) == frow) & (lax.shift_right_logical(fcl, 3) <= t)
    fs = jnp.where(fmask, fs, NEG_FILL)
    ftop = jnp.max(fs, axis=1, keepdims=True)
    fw = jnp.where(fmask, jnp.exp(fs - ftop), 0.0).astype(BF16)
    ftot = jnp.sum(fw.astype(F32), axis=1, keepdims=True)
    facc = jnp.dot(fw, nv, preferred_element_type=F32)

    ra[0] = pa[y]
    for c in ca:
        c.wait_recv()
    tiles = [join3(ra[d, 16].astype(F32)) for d in range(4)]
    peak = jnp.maximum(jnp.maximum(tiles[0], tiles[1]), jnp.maximum(tiles[2], tiles[3]))
    fac = [jnp.exp(v - peak) for v in tiles]
    total = sum(pltpu.roll(f, 48, 1) * v for f, v in zip(fac, tiles))
    merged = jnp.where(lane < 16, peak, jnp.where((lane >= 48) & (lane < 64), total, 0.0))
    merged = split3(merged)
    for i in range(16):
        acc = sum(fac[d][:, i:i + 1] * ra[d, i].astype(F32) for d in range(4))
        zt = 2 * (i % 8) + i // 8
        pb[zt, 0] = acc.astype(BF16)
        pb[zt, 1] = merged

    cb = []
    for d in range(1, 16):
        zt = lax.rem(z + d, 16)
        cb.append(remote(pb.at[zt], rb.at[d], b_s.at[d], b_r.at[d], (at(y, zt), q)))
    send(cb)
    rb[0] = pb[z]
    for c in cb:
        c.wait_recv()
    own = kb * 8 + tg
    lane3 = lax.broadcasted_iota(jnp.int32, (16, 8, 128), 2)
    mine = (lane3 & 15) == own
    ml = rb[:, 1].astype(F32)
    m = jnp.sum(jnp.where(mine & (lane3 < 48), ml, 0.0), axis=2, keepdims=True)
    l = jnp.sum(jnp.where(mine & (lane3 >= 48), ml, 0.0), axis=2, keepdims=True)
    peak = jnp.maximum(jnp.max(m, axis=0), ftop)
    f = jnp.exp(m - peak[None])
    ff = jnp.exp(ftop - peak)
    total = jnp.sum(f * l, axis=0) + ff * ftot
    acc = jnp.sum(f * rb[:, 0].astype(F32), axis=0) + ff * facc
    attn = (acc / total).astype(BF16).astype(F32)
    stream = (res_v[...].astype(F32) + attn).astype(BF16)
    x_v[q, t, :, gcol] = stream

    cc = []
    for d in range(1, 8):
        zt = lax.rem(z + 2 * d, 16)
        ref = x_v.at[q, t, :, gcol]
        cc.append(remote(ref, ref, c_s.at[d], c_r.at[d], (at(y, zt), q)))
    send(cc)
    for c in cc:
        c.wait_recv()
    cd = []
    for d in range(1, 8):
        ref = x_v.at[q]
        cd.append(remote(ref, ref, d_s.at[d], d_r.at[d], (s, lax.rem(q + d, 8))))
    send(cd)
    for f8 in range(8):
        copy = remote(ws.at[f8], wr.at[f8], ws_s.at[f8], ws_r.at[f8], (s, q))

        @pl.when(8 * kb + f8 != z)
        def _():
            copy.wait_recv()
    for c in cd:
        c.wait_recv()

    xf = x_v[...].astype(F32).reshape(256, 256)
    square = jnp.sum(xf * xf, axis=1, keepdims=True)
    xg = (xf * gain_v[...].astype(F32)).astype(BF16)
    gu = jnp.dot(xg, wr[:, :, 0:256].reshape(256, 256), preferred_element_type=F32)
    hi = square.astype(BF16).astype(F32)
    lane2 = lax.broadcasted_iota(jnp.int32, (256, 256), 1)
    gu = jnp.where(lane2 == 96, hi, jnp.where(lane2 == 97, square - hi, gu))
    pp[...] = gu.astype(BF16).reshape(8, 32, 256)
    k_targets = []
    for dy in range(4):
        for dk in range(2):
            if dy or dk:
                yt = lax.rem(y + dy, 4)
                zt = zpair if dk else z
                kt = yt * 2 + (1 - kb if dk else kb)
                k_targets.append((2 * dy + dk, kt, (at(yt, zt), q)))
    ce = [remote(pp.at[kt], rp.at[d], e_s.at[d], e_r.at[d], peer) for d, kt, peer in k_targets]
    send(ce)
    rp[0] = pp[k]
    for c in ce:
        c.wait_recv()
    gu = jnp.sum(rp[...].astype(F32), axis=0)
    lane32 = lax.broadcasted_iota(jnp.int32, (32, 128), 1)
    gate, up = gu[:, :128], gu[:, 128:]
    square = jnp.sum(jnp.where((lane32 == 96) | (lane32 == 97), gate, 0.0), axis=1, keepdims=True)
    norm = lax.rsqrt(square * (1.0 / 2048) + EPSILON)
    gate = gate * norm
    up = up * norm
    hidden = gate / (1.0 + jnp.exp(-gate)) * up
    hh[k] = jnp.where(lane32 < 96, hidden, 0.0).astype(BF16)
    cf = []
    for d, kt, peer in k_targets:
        cf.append(remote(hh.at[k], hh.at[k], f_s.at[d], f_r.at[d], peer))
    send(cf)
    for c in cf:
        c.wait_recv()

    down = lax.dot_general(
        hh[...].reshape(256, 128), wr[:, :, 256:384].reshape(256, 128), NT, preferred_element_type=F32
    )
    dd[...] = down.astype(BF16).reshape(8, 32, 256)
    cg = []
    for d in range(1, 8):
        qt = lax.rem(q + d, 8)
        cg.append(remote(dd.at[qt], rd.at[d], g_s.at[d], g_r.at[d], (s, qt)))
    send(cg)
    rd[0] = dd[q]
    for c in cg:
        c.wait_recv()
    down = jnp.sum(rd[...].astype(F32), axis=0)
    for i in range(8):
        tt, gg = i // 2, i % 2
        ee[i] = down[8 * tt:8 * tt + 8, 128 * gg:128 * gg + 128].astype(BF16)
    ch = []
    for d in range(1, 8):
        zt = lax.rem(z + 2 * d, 16)
        ch.append(remote(ee.at[lax.div(zt, 2)], re.at[d], h_s.at[d], h_r.at[d], (at(y, zt), q)))
    send(ch)
    re[0] = ee[tg]
    for c in ch:
        c.wait_recv()
    final = stream.astype(F32) + jnp.sum(re[...].astype(F32), axis=0)
    out[t, :, hcol] = final.astype(BF16)

    ci = []
    for d in range(1, 16):
        ref = out.at[t, :, hcol]
        ci.append(remote(ref, ref, i_s.at[d], i_r.at[d], (at(y, lax.rem(z + d, 16)), q)))
    send(ci)
    for c in ci:
        c.wait_recv()
    cj = []
    for d in range(1, 4):
        ref = out.at[:, :, pl.ds(pl.multiple_of(y * 512, 512), 512)]
        cj.append(remote(ref, ref, j_s.at[d], j_r.at[d], (at(lax.rem(y + d, 4), z), q)))
    send(cj)
    for c in cj:
        c.wait_recv()

    for c in sent:
        c.wait_send()
    for j in range(8):
        zt = 2 * j + zhi
        copy = remote(ws.at[j], wr.at[zlo], ws_s.at[j], ws_r.at[zlo], (at(y, zt), q))

        @pl.when(zt != z)
        def _():
            copy.wait_send()


def step(q, nk, nv, kc, vc, cache_len, resid, gain, w_gate, w_up, w_down):
    hbm = pl.BlockSpec(memory_space=pl.ANY)
    dma = lambda n: pltpu.SemaphoreType.DMA((n,))
    vm = pltpu.VMEM
    sems = []
    for n in (8, 4, 16, 8, 8, 8, 8, 8, 8, 16, 4):
        sems += [dma(n), dma(n)]
    return pl.pallas_call(
        kernel,
        out_shape=jax.ShapeDtypeStruct((4, 8, 2048), BF16),
        in_specs=[hbm] * 5 + [pl.BlockSpec(memory_space=pltpu.SMEM)] + [hbm] * 5,
        out_specs=pl.BlockSpec(memory_space=pltpu.VMEM),
        scratch_shapes=[
            vm((4, 8, 2048), BF16), vm((4, 8, 128), BF16), vm((4, 8, 128), BF16),
            vm((8, 32, 1024), BF16), vm((8, 32, 1024), BF16), vm((8, 128), BF16), vm((1, 256), BF16),
            vm((32, 768), BF16), vm((32, 768), BF16), vm((768, 32), BF16),
            vm((8, 32, 384), BF16), vm((8, 32, 384), BF16),
            vm((4, 17, 8, 128), BF16), vm((4, 17, 8, 128), BF16),
            vm((16, 2, 8, 128), BF16), vm((16, 2, 8, 128), BF16),
            vm((8, 4, 8, 256), BF16),
            vm((8, 32, 256), BF16), vm((8, 32, 256), BF16),
            vm((8, 32, 128), BF16),
            vm((8, 32, 256), BF16), vm((8, 32, 256), BF16),
            vm((8, 8, 128), BF16), vm((8, 8, 128), BF16),
            dma(10),
        ] + sems,
        compiler_params=pltpu.CompilerParams(
            collective_id=0, has_side_effects=True, vmem_limit_bytes=16 * 1024 * 1024
        ),
    )(q, nk, nv, kc, vc, cache_len, resid, gain.reshape(1, 2048), w_gate, w_up, w_down)


def solution(mesh):
    placed = (
        P(None, "req", None),
        P(None, "req", None),
        P(None, "req", None),
        P("req", "seq", None),
        P("req", "seq", None),
        P("req"),
        P(None, "req", None),
        P(),
        P("seq", "req"),
        P("seq", "req"),
        P("req", "seq"),
    )
    return jax.shard_map(step, mesh=mesh, in_specs=placed, out_specs=P(None, "req", None), check_vma=False)
```

```python
import functools
import math

import jax
import jax.numpy as jnp
from jax import lax
from jax.experimental import pallas as pl
from jax.experimental.pallas import tpu as pltpu
from jax.sharding import PartitionSpec as P

NEG_FILL = -1e30
EPSILON = 1e-06
F32 = jnp.float32
BF16 = jnp.bfloat16
NT = (((1,), (1,)), ((), ()))
SCALE = 1.0 / math.sqrt(128)


def split3(x):
    hi = x.astype(BF16).astype(F32)
    rest = x - hi
    mid = rest.astype(BF16).astype(F32)
    low = (rest - mid).astype(BF16).astype(F32)
    return (hi + pltpu.roll(mid, 16, 1) + pltpu.roll(low, 32, 1)).astype(BF16)


def join3(x):
    return x + pltpu.roll(x, 112, 1) + pltpu.roll(x, 96, 1)


def kernel(
    q_h, nk_h, nv_h, k_h, v_h, len_s, resid_h, gain_h, wg_h, wu_h, wd_h,
    out,
    q_v, nk_v, nv_v, k_v, v_v, res_v, gain_v, wg_v, wu_v, wd_v,
    ws, wr, pa, ra, pb, rb, x_v, pp, rp, hh, dd, rd, ee, re,
    lsem,
    ws_s, ws_r, a_s, a_r, b_s, b_r, c_s, c_r, d_s, d_r, e_s, e_r, f_s, f_r, g_s, g_r, h_s, h_r,
):
    s = lax.axis_index("seq")
    q = lax.axis_index("req")
    y = lax.div(s, 16)
    z = lax.rem(s, 16)
    kb = lax.rem(z, 2)
    tg = lax.div(z, 2)
    k = y * 2 + kb
    zpair = z + 1 - 2 * kb
    zhi = lax.div(z, 8)
    zlo = lax.rem(z, 8)

    def at(yy, zz):
        return yy * 16 + zz

    k_peers = []
    for dy in range(4):
        for dk in range(2):
            if dy or dk:
                yt = lax.rem(y + dy, 4)
                kt = yt * 2 + (1 - kb if dk else kb)
                k_peers.append((2 * dy + dk, kt, (at(yt, zpair if dk else z), q)))
    t_peers = []
    for d in range(1, 8):
        zt = lax.rem(z + 2 * d, 16)
        t_peers.append((d, lax.div(zt, 2), (at(y, zt), q)))
    q_peers = [(d, lax.rem(q + d, 8), (s, lax.rem(q + d, 8))) for d in range(1, 8)]
    odd_z = [(at(y, lax.rem(zpair + 2 * d, 16)), q) for d in range(1, 8)]

    barrier = pltpu.get_barrier_semaphore()
    for peer in [p[2] for p in k_peers + t_peers + q_peers] + odd_z:
        pl.semaphore_signal(barrier, inc=1, device_id=peer, device_id_type=pl.DeviceIdType.MESH)

    kcol = pl.ds(pl.multiple_of(k * 128, 128), 128)
    fcol = pl.ds(pl.multiple_of(k * 256, 256), 256)
    loads = [
        (wg_h, wg_v), (wu_h, wu_v), (wd_h, wd_v), (q_h, q_v), (k_h, k_v), (v_h, v_v),
        (nk_h.at[:, :, kcol], nk_v), (nv_h.at[:, :, kcol], nv_v),
        (resid_h.at[:, :, fcol], res_v), (gain_h, gain_v),
    ]
    loads = [pltpu.make_async_copy(a, b, lsem.at[i]) for i, (a, b) in enumerate(loads)]
    for c in loads:
        c.start()

    def remote(src, dst, ssem, rsem, peer):
        return pltpu.make_async_remote_copy(
            src_ref=src, dst_ref=dst, send_sem=ssem, recv_sem=rsem,
            device_id=peer, device_id_type=pl.DeviceIdType.MESH,
        )

    sent = []

    def send(copies):
        for c in copies:
            c.start()
        sent.extend(copies)
        return copies

    for c in loads[:3]:
        c.wait()
    whole = [wg_v[...].astype(F32), wu_v[...].astype(F32), wd_v[...].astype(F32)]
    keep = lax.broadcasted_iota(jnp.int32, (32, 128), 1) < 96
    for j in range(8):
        base, off = (96 * j) // 128 * 128, (96 * j) % 128
        for i, w in enumerate(whole):
            if off + 96 <= 128:
                piece = w[:, base:base + 128]
                if off:
                    piece = pltpu.roll(piece, 128 - off, 1)
            else:
                piece = pltpu.roll(w[:, base:base + 256], 256 - off, 1)[:, :128]
            ws[j, :, 128 * i:128 * i + 128] = jnp.where(keep, piece, 0.0).astype(BF16)

    for c in loads[3:6]:
        c.wait()
    row = lax.broadcasted_iota(jnp.int32, (64, 256), 0) & 7
    col = lax.broadcasted_iota(jnp.int32, (64, 256), 1)
    limit = jnp.zeros((64, 256), jnp.int32)
    for r in range(8):
        limit = jnp.where(row == r, len_s[r], limit)
    mask = (lax.shift_right_logical(col, 5) == row) & ((col & 31) + s * 32 < limit)
    lane = lax.broadcasted_iota(jnp.int32, (8, 128), 1)

    def stats(top, tot):
        tile = jnp.zeros((8, 128), F32)
        for i in range(8):
            tile = jnp.where(lane == i, top[8 * i:8 * i + 8], tile)
            tile = jnp.where(lane == 48 + i, tot[8 * i:8 * i + 8], tile)
        return tile

    for kv in range(8):
        qk = jnp.concatenate(
            [
                q_v[tt, :, 128 * (2 * kv + gg):128 * (2 * kv + gg) + 128].astype(F32)
                for tt in range(4) for gg in range(2)
            ],
            axis=0,
        ).astype(BF16)
        keys = k_v[:, :, 128 * kv:128 * kv + 128].reshape(256, 128)
        vals = v_v[:, :, 128 * kv:128 * kv + 128].reshape(256, 128)
        sc = lax.dot_general(qk, keys, NT, preferred_element_type=F32) * SCALE
        sc = jnp.where(mask, sc, NEG_FILL)
        top = jnp.max(sc, axis=1, keepdims=True)
        w = jnp.where(mask, jnp.exp(sc - top), 0.0).astype(BF16)
        tot = jnp.sum(w.astype(F32), axis=1, keepdims=True)
        acc = jnp.dot(w, vals, preferred_element_type=F32).astype(BF16)
        pa[kv, 0:8] = acc.reshape(8, 8, 128)
        pa[kv, 8] = split3(stats(top, tot))

    pl.semaphore_wait(barrier, 28)

    ca = send([remote(pa.at[kt], ra.at[d], a_s.at[d], a_r.at[d], peer) for d, kt, peer in k_peers])

    for j in range(8):
        zt = 2 * j + zhi
        copy = remote(ws.at[j], wr.at[zlo], ws_s.at[j], ws_r.at[zlo], (at(y, zt), q))

        @pl.when(zt != z)
        def _():
            copy.start()

        @pl.when(zt == z)
        def _():
            wr[zlo] = ws[j]

    for c in loads[6:]:
        c.wait()
    qf = jnp.concatenate(
        [
            q_v[tt, :, pl.ds(pl.multiple_of(k * 256 + 128 * gg, 128), 128)].astype(F32)
            for tt in range(4) for gg in range(2)
        ],
        axis=0,
    ).astype(BF16)
    nk = nk_v[...].astype(F32).reshape(32, 128).astype(BF16)
    nv = nv_v[...].astype(F32).reshape(32, 128).astype(BF16)
    fs = lax.dot_general(qf, nk, NT, preferred_element_type=F32) * SCALE
    frow = lax.broadcasted_iota(jnp.int32, (64, 32), 0)
    fcl = lax.broadcasted_iota(jnp.int32, (64, 32), 1)
    fmask = ((fcl & 7) == (frow & 7)) & (lax.shift_right_logical(fcl, 3) <= lax.shift_right_logical(frow, 4))
    fs = jnp.where(fmask, fs, NEG_FILL)
    ftop = jnp.max(fs, axis=1, keepdims=True)
    fw = jnp.where(fmask, jnp.exp(fs - ftop), 0.0).astype(BF16)
    ftot = jnp.sum(fw.astype(F32), axis=1, keepdims=True)
    facc = jnp.dot(fw, nv, preferred_element_type=F32)
    fstat = stats(ftop, ftot)

    def merge(parts):
        peak = functools.reduce(jnp.maximum, parts)
        fac = [jnp.exp(v - peak) for v in parts]
        total = sum(pltpu.roll(f, 48, 1) * v for f, v in zip(fac, parts))
        return peak, fac, total

    ra[0] = pa[k]
    for c in ca:
        c.wait_recv()
    peak, fac, total = merge([join3(ra[d, 8].astype(F32)) for d in range(8)])
    for i in range(8):
        pb[i] = sum(fac[d][:, i:i + 1] * ra[d, i].astype(F32) for d in range(8)).astype(BF16)
    pb[8] = split3(jnp.where(lane < 8, peak, jnp.where((lane >= 48) & (lane < 56), total, 0.0)))

    cb = send([remote(pb, rb.at[tg], b_s.at[d], b_r.at[d], peer) for d, _, peer in t_peers])
    rb[tg] = pb[...]
    for c in cb:
        c.wait_recv()
    _, fac, total = merge([join3(rb[d, 8].astype(F32)) for d in range(8)] + [fstat])
    inverse = pltpu.roll(total, 80, 1)
    for i in range(8):
        acc = sum(fac[d][:, i:i + 1] * rb[d, i].astype(F32) for d in range(8))
        acc = acc + fac[8][:, i:i + 1] * facc[8 * i:8 * i + 8]
        attn = (acc / inverse[:, i:i + 1]).astype(BF16).astype(F32)
        tt, gg = i // 2, i % 2
        x_v[q, tt, :, 128 * gg:128 * gg + 128] = (
            res_v[tt, :, 128 * gg:128 * gg + 128].astype(F32) + attn
        ).astype(BF16)

    cd = send([remote(x_v.at[q], x_v.at[q], d_s.at[d], d_r.at[d], peer) for d, _, peer in q_peers])
    for f8 in range(8):
        copy = remote(ws.at[f8], wr.at[f8], ws_s.at[f8], ws_r.at[f8], (s, q))

        @pl.when(8 * kb + f8 != z)
        def _():
            copy.wait_recv()
    for c in cd:
        c.wait_recv()

    xf = x_v[...].astype(F32).reshape(256, 256)
    square = jnp.sum(xf * xf, axis=1, keepdims=True)
    xg = (xf * gain_v[fcol].astype(F32).reshape(1, 256)).astype(BF16)
    gu = jnp.dot(xg, wr[:, :, 0:256].reshape(256, 256), preferred_element_type=F32)
    hi = square.astype(BF16).astype(F32)
    lane2 = lax.broadcasted_iota(jnp.int32, (256, 256), 1)
    gu = jnp.where(lane2 == 96, hi, jnp.where(lane2 == 97, square - hi, gu))
    pp[...] = gu.astype(BF16).reshape(8, 32, 256)
    ce = send([remote(pp.at[kt], rp.at[d], e_s.at[d], e_r.at[d], peer) for d, kt, peer in k_peers])
    rp[0] = pp[k]
    for c in ce:
        c.wait_recv()
    gu = jnp.sum(rp[...].astype(F32), axis=0)
    lane32 = lax.broadcasted_iota(jnp.int32, (32, 128), 1)
    gate, up = gu[:, :128], gu[:, 128:]
    square = jnp.sum(jnp.where((lane32 == 96) | (lane32 == 97), gate, 0.0), axis=1, keepdims=True)
    norm = lax.rsqrt(square * (1.0 / 2048) + EPSILON)
    gate = gate * norm
    up = up * norm
    hidden = gate / (1.0 + jnp.exp(-gate)) * up
    hh[k] = jnp.where(lane32 < 96, hidden, 0.0).astype(BF16)
    cf = send([remote(hh.at[k], hh.at[k], f_s.at[d], f_r.at[d], peer) for d, _, peer in k_peers])
    for c in cf:
        c.wait_recv()

    down = lax.dot_general(
        hh[...].reshape(256, 128), wr[:, :, 256:384].reshape(256, 128), NT, preferred_element_type=F32
    )
    dd[...] = down.astype(BF16).reshape(8, 32, 256)
    cg = send([remote(dd.at[qt], rd.at[d], g_s.at[d], g_r.at[d], peer) for d, qt, peer in q_peers])
    rd[0] = dd[q]
    for c in cg:
        c.wait_recv()
    ee[...] = jnp.sum(rd[...].astype(F32), axis=0).astype(BF16)
    ch = send([remote(ee, re.at[tg], h_s.at[d], h_r.at[d], peer) for d, _, peer in t_peers])
    re[tg] = ee[...]
    for c in ch:
        c.wait_recv()
    final = x_v[q].astype(F32) + jnp.sum(re[...].astype(F32), axis=0).reshape(4, 8, 256)
    out[:, :, fcol] = final.astype(BF16)

    ci = send([remote(out.at[:, :, fcol], out.at[:, :, fcol], c_s.at[d], c_r.at[d], peer) for d, _, peer in k_peers])
    for c in ci:
        c.wait_recv()

    for c in sent:
        c.wait_send()
    for j in range(8):
        zt = 2 * j + zhi
        copy = remote(ws.at[j], wr.at[zlo], ws_s.at[j], ws_r.at[zlo], (at(y, zt), q))

        @pl.when(zt != z)
        def _():
            copy.wait_send()


def step(q, nk, nv, kc, vc, cache_len, resid, gain, w_gate, w_up, w_down):
    hbm = pl.BlockSpec(memory_space=pl.ANY)
    dma = lambda n: pltpu.SemaphoreType.DMA((n,))
    vm = pltpu.VMEM
    sems = []
    for _ in range(9):
        sems += [dma(8), dma(8)]
    return pl.pallas_call(
        kernel,
        out_shape=jax.ShapeDtypeStruct((4, 8, 2048), BF16),
        in_specs=[hbm] * 5 + [pl.BlockSpec(memory_space=pltpu.SMEM)] + [hbm] * 5,
        out_specs=pl.BlockSpec(memory_space=pltpu.VMEM),
        scratch_shapes=[
            vm((4, 8, 2048), BF16), vm((4, 8, 128), BF16), vm((4, 8, 128), BF16),
            vm((8, 32, 1024), BF16), vm((8, 32, 1024), BF16), vm((4, 8, 256), BF16), vm((2048,), BF16),
            vm((32, 768), BF16), vm((32, 768), BF16), vm((32, 768), BF16),
            vm((8, 32, 384), BF16), vm((8, 32, 384), BF16),
            vm((8, 9, 8, 128), BF16), vm((8, 9, 8, 128), BF16),
            vm((9, 8, 128), BF16), vm((8, 9, 8, 128), BF16),
            vm((8, 4, 8, 256), BF16),
            vm((8, 32, 256), BF16), vm((8, 32, 256), BF16),
            vm((8, 32, 128), BF16),
            vm((8, 32, 256), BF16), vm((8, 32, 256), BF16),
            vm((32, 256), BF16), vm((8, 32, 256), BF16),
            dma(10),
        ] + sems,
        compiler_params=pltpu.CompilerParams(
            collective_id=0, has_side_effects=True, vmem_limit_bytes=60 * 1024 * 1024
        ),
    )(q, nk, nv, kc, vc, cache_len, resid, gain, w_gate, w_up, w_down.T)


def solution(mesh):
    placed = (
        P(None, "req", None),
        P(None, "req", None),
        P(None, "req", None),
        P("req", "seq", None),
        P("req", "seq", None),
        P("req"),
        P(None, "req", None),
        P(),
        P("seq", "req"),
        P("seq", "req"),
        P("req", "seq"),
    )
    return jax.shard_map(step, mesh=mesh, in_specs=placed, out_specs=P(None, "req", None), check_vma=False)
```

```python
import functools
import math

import jax
import jax.numpy as jnp
from jax import lax
from jax.experimental import pallas as pl
from jax.experimental.pallas import tpu as pltpu
from jax.sharding import PartitionSpec as P

NEG_FILL = -1e30
EPSILON = 1e-06
F32 = jnp.float32
BF16 = jnp.bfloat16
NT = (((1,), (1,)), ((), ()))
SCALE = 1.0 / math.sqrt(128)


def split3(x):
    hi = x.astype(BF16).astype(F32)
    rest = x - hi
    mid = rest.astype(BF16).astype(F32)
    low = (rest - mid).astype(BF16).astype(F32)
    return (hi + pltpu.roll(mid, 16, 1) + pltpu.roll(low, 32, 1)).astype(BF16)


def join3(x):
    return x + pltpu.roll(x, 112, 1) + pltpu.roll(x, 96, 1)


def kernel(
    q_h, nk_h, nv_h, k_h, v_h, len_s, resid_h, gain_h, wg_h, wu_h, wd_h,
    out,
    q_v, nk_v, nv_v, k_v, v_v, res_v, gain_v, wg_v, wu_v, wd_v,
    ws, wr, pa, ra, pb, rb, x_v, pp, rp, hh, dd, rd, ee, re,
    lsem,
    ws_s, ws_r, a_s, a_r, b_s, b_r, c_s, c_r, d_s, d_r, e_s, e_r, f_s, f_r, g_s, g_r, h_s, h_r,
):
    s = lax.axis_index("seq")
    q = lax.axis_index("req")
    y = lax.div(s, 16)
    z = lax.rem(s, 16)
    kb = lax.rem(z, 2)
    k = y * 2 + kb
    zpair = z + 1 - 2 * kb
    zh = lax.div(z, 4)
    zl = lax.rem(z, 4)
    half = lax.div(zl, 2)
    zhi = lax.div(z, 8)
    zlo = lax.rem(z, 8)

    def at(yy, zz):
        return yy * 16 + zz

    a_peers = []
    for dy in range(4):
        for dz in range(4):
            if dy or dz:
                yt, zt = lax.rem(y + dy, 4), lax.rem(zl + dz, 4)
                kt, ht = yt * 2 + lax.rem(zt, 2), lax.div(zt, 2)
                a_peers.append((4 * dy + dz, kt, ht, (at(yt, 4 * zh + zt), q)))
    z_peers = [(d, (at(y, lax.rem(z + 4 * d, 16)), q)) for d in range(1, 4)]
    c_peers = []
    for dq in range(8):
        for dh in range(2):
            if dq or dh:
                qt = lax.rem(q + dq, 8)
                ht = 1 - half if dh else half
                c_peers.append((2 * dq + dh, qt, ht, (at(y, 4 * zh + 2 * ht + kb), qt)))
    k_peers = []
    for dy in range(4):
        for dk in range(2):
            if dy or dk:
                yt = lax.rem(y + dy, 4)
                kt = yt * 2 + (1 - kb if dk else kb)
                k_peers.append((2 * dy + dk, kt, (at(yt, zpair if dk else z), q)))
    rest = [(at(y, 4 * lax.rem(zh + i, 4) + lax.rem(zl + j, 4)), q) for i in range(1, 4) for j in range(1, 4)]

    kcol = pl.ds(pl.multiple_of(k * 128, 128), 128)
    fcol = pl.ds(pl.multiple_of(k * 256, 256), 256)
    loads = [
        (wg_h, wg_v), (wu_h, wu_v), (wd_h, wd_v), (q_h, q_v), (k_h, k_v), (v_h, v_v),
        (nk_h.at[:, :, kcol], nk_v), (nv_h.at[:, :, kcol], nv_v),
        (resid_h.at[pl.ds(2 * half, 2), :, fcol], res_v), (gain_h, gain_v),
    ]
    loads = [pltpu.make_async_copy(a, b, lsem.at[i]) for i, (a, b) in enumerate(loads)]
    for c in loads:
        c.start()

    barrier = pltpu.get_barrier_semaphore()
    greeted = [p[-1] for p in a_peers + z_peers + c_peers if p is not c_peers[0]] + rest
    for peer in greeted:
        pl.semaphore_signal(barrier, inc=1, device_id=peer, device_id_type=pl.DeviceIdType.MESH)

    def remote(src, dst, ssem, rsem, peer):
        return pltpu.make_async_remote_copy(
            src_ref=src, dst_ref=dst, send_sem=ssem, recv_sem=rsem,
            device_id=peer, device_id_type=pl.DeviceIdType.MESH,
        )

    sent = []

    def send(copies):
        for c in copies:
            c.start()
        sent.extend(copies)
        return copies

    for c in loads[:3]:
        c.wait()
    whole = [wg_v[...].astype(F32), wu_v[...].astype(F32), wd_v[...].astype(F32)]
    keep = lax.broadcasted_iota(jnp.int32, (32, 128), 1) < 96
    for j in range(8):
        base, off = (96 * j) // 128 * 128, (96 * j) % 128
        for i, w in enumerate(whole):
            if off + 96 <= 128:
                piece = w[:, base:base + 128]
                if off:
                    piece = pltpu.roll(piece, 128 - off, 1)
            else:
                piece = pltpu.roll(w[:, base:base + 256], 256 - off, 1)[:, :128]
            ws[j, :, 128 * i:128 * i + 128] = jnp.where(keep, piece, 0.0).astype(BF16)

    for c in loads[3:6]:
        c.wait()
    row = lax.broadcasted_iota(jnp.int32, (64, 256), 0) & 7
    col = lax.broadcasted_iota(jnp.int32, (64, 256), 1)
    limit = jnp.zeros((64, 256), jnp.int32)
    for r in range(8):
        limit = jnp.where(row == r, len_s[r], limit)
    mask = (lax.shift_right_logical(col, 5) == row) & ((col & 31) + s * 32 < limit)
    lane = lax.broadcasted_iota(jnp.int32, (8, 128), 1)

    def stats(top, tot):
        tile = jnp.zeros((8, 128), F32)
        for i in range(4):
            tile = jnp.where(lane == i, top[8 * i:8 * i + 8], tile)
            tile = jnp.where(lane == 48 + i, tot[8 * i:8 * i + 8], tile)
        return tile

    for kv in range(8):
        qk = jnp.concatenate(
            [
                q_v[tt, :, 128 * (2 * kv + gg):128 * (2 * kv + gg) + 128].astype(F32)
                for tt in range(4) for gg in range(2)
            ],
            axis=0,
        ).astype(BF16)
        keys = k_v[:, :, 128 * kv:128 * kv + 128].reshape(256, 128)
        vals = v_v[:, :, 128 * kv:128 * kv + 128].reshape(256, 128)
        sc = lax.dot_general(qk, keys, NT, preferred_element_type=F32) * SCALE
        sc = jnp.where(mask, sc, NEG_FILL)
        top = jnp.max(sc, axis=1, keepdims=True)
        w = jnp.where(mask, jnp.exp(sc - top), 0.0).astype(BF16)
        tot = jnp.sum(w.astype(F32), axis=1, keepdims=True)
        acc = jnp.dot(w, vals, preferred_element_type=F32).astype(BF16)
        for h in range(2):
            pa[kv, h, 0:4] = acc[32 * h:32 * h + 32].reshape(4, 8, 128)
            pa[kv, h, 4] = split3(stats(top[32 * h:32 * h + 32], tot[32 * h:32 * h + 32]))

    pl.semaphore_wait(barrier, len(greeted))

    ca = send([remote(pa.at[kt, ht], ra.at[d], a_s.at[d], a_r.at[d], peer) for d, kt, ht, peer in a_peers])

    for j in range(8):
        zt = 2 * j + zhi
        copy = remote(ws.at[j], wr.at[zlo], ws_s.at[j], ws_r.at[zlo], (at(y, zt), q))

        @pl.when(zt != z)
        def _():
            copy.start()

        @pl.when(zt == z)
        def _():
            wr[zlo] = ws[j]

    for c in loads[6:]:
        c.wait()
    qf = jnp.concatenate(
        [
            q_v[2 * half + tt, :, pl.ds(pl.multiple_of(k * 256 + 128 * gg, 128), 128)].astype(F32)
            for tt in range(2) for gg in range(2)
        ],
        axis=0,
    ).astype(BF16)
    nk = nk_v[...].astype(F32).reshape(32, 128).astype(BF16)
    nv = nv_v[...].astype(F32).reshape(32, 128).astype(BF16)
    fs = lax.dot_general(qf, nk, NT, preferred_element_type=F32) * SCALE
    frow = lax.broadcasted_iota(jnp.int32, (32, 32), 0)
    fcl = lax.broadcasted_iota(jnp.int32, (32, 32), 1)
    fmask = ((fcl & 7) == (frow & 7)) & (lax.shift_right_logical(fcl, 3) <= lax.shift_right_logical(frow, 4) + 2 * half)
    fs = jnp.where(fmask, fs, NEG_FILL)
    ftop = jnp.max(fs, axis=1, keepdims=True)
    fw = jnp.where(fmask, jnp.exp(fs - ftop), 0.0).astype(BF16)
    ftot = jnp.sum(fw.astype(F32), axis=1, keepdims=True)
    facc = jnp.dot(fw, nv, preferred_element_type=F32)
    fstat = stats(ftop, ftot)

    def merge(parts):
        peak = functools.reduce(jnp.maximum, parts)
        fac = [jnp.exp(v - peak) for v in parts]
        total = sum(pltpu.roll(f, 48, 1) * v for f, v in zip(fac, parts))
        return peak, fac, total

    ra[0] = pa[k, half]
    for c in ca:
        c.wait_recv()
    peak, fac, total = merge([join3(ra[d, 4].astype(F32)) for d in range(16)])
    for i in range(4):
        pb[i] = sum(fac[d][:, i:i + 1] * ra[d, i].astype(F32) for d in range(16)).astype(BF16)
    pb[4] = split3(jnp.where(lane < 4, peak, jnp.where((lane >= 48) & (lane < 52), total, 0.0)))

    cb = send([remote(pb, rb.at[zh], b_s.at[d], b_r.at[d], peer) for d, peer in z_peers])
    rb[zh] = pb[...]
    for c in cb:
        c.wait_recv()
    _, fac, total = merge([join3(rb[d, 4].astype(F32)) for d in range(4)] + [fstat])
    inverse = pltpu.roll(total, 80, 1)
    for i in range(4):
        acc = sum(fac[d][:, i:i + 1] * rb[d, i].astype(F32) for d in range(4))
        acc = acc + fac[4][:, i:i + 1] * facc[8 * i:8 * i + 8]
        attn = (acc / inverse[:, i:i + 1]).astype(BF16).astype(F32)
        tt, gg = i // 2, i % 2
        x_v[q, 2 * half + tt, :, 128 * gg:128 * gg + 128] = (
            res_v[tt, :, 128 * gg:128 * gg + 128].astype(F32) + attn
        ).astype(BF16)

    mine = x_v.at[q, pl.ds(2 * half, 2)]
    cd = send([remote(mine, mine, d_s.at[d], d_r.at[d], peer) for d, _, _, peer in c_peers])
    for f8 in range(8):
        copy = remote(ws.at[f8], wr.at[f8], ws_s.at[f8], ws_r.at[f8], (s, q))

        @pl.when(8 * kb + f8 != z)
        def _():
            copy.wait_recv()
    for c in cd:
        c.wait_recv()

    xf = x_v[...].astype(F32).reshape(256, 256)
    square = jnp.sum(xf * xf, axis=1, keepdims=True)
    xg = (xf * gain_v[fcol].astype(F32).reshape(1, 256)).astype(BF16)
    gu = jnp.dot(xg, wr[:, :, 0:256].reshape(256, 256), preferred_element_type=F32)
    hi = square.astype(BF16).astype(F32)
    lane2 = lax.broadcasted_iota(jnp.int32, (256, 256), 1)
    gu = jnp.where(lane2 == 96, hi, jnp.where(lane2 == 97, square - hi, gu))
    pp[...] = gu.astype(BF16).reshape(8, 32, 256)
    ce = send([remote(pp.at[kt], rp.at[d], e_s.at[d], e_r.at[d], peer) for d, kt, peer in k_peers])
    rp[0] = pp[k]
    for c in ce:
        c.wait_recv()
    gu = jnp.sum(rp[...].astype(F32), axis=0)
    lane32 = lax.broadcasted_iota(jnp.int32, (32, 128), 1)
    gate, up = gu[:, :128], gu[:, 128:]
    square = jnp.sum(jnp.where((lane32 == 96) | (lane32 == 97), gate, 0.0), axis=1, keepdims=True)
    norm = lax.rsqrt(square * (1.0 / 2048) + EPSILON)
    gate = gate * norm
    up = up * norm
    hidden = gate / (1.0 + jnp.exp(-gate)) * up
    hh[k] = jnp.where(lane32 < 96, hidden, 0.0).astype(BF16)
    cf = send([remote(hh.at[k], hh.at[k], f_s.at[d], f_r.at[d], peer) for d, _, peer in k_peers])
    for c in cf:
        c.wait_recv()

    down = lax.dot_general(
        hh[...].reshape(256, 128), wr[:, :, 256:384].reshape(256, 128), NT, preferred_element_type=F32
    )
    dd[...] = down.astype(BF16).reshape(8, 2, 16, 256)
    cg = send([remote(dd.at[qt, ht], rd.at[d], g_s.at[d], g_r.at[d], peer) for d, qt, ht, peer in c_peers])
    rd[0] = dd[q, half]
    for c in cg:
        c.wait_recv()
    ee[...] = jnp.sum(rd[...].astype(F32), axis=0).astype(BF16)
    ch = send([remote(ee, re.at[zh], h_s.at[d], h_r.at[d], peer) for d, peer in z_peers])
    re[zh] = ee[...]
    for c in ch:
        c.wait_recv()
    final = mine[...].astype(F32) + jnp.sum(re[...].astype(F32), axis=0).reshape(2, 8, 256)
    piece = out.at[pl.ds(2 * half, 2), :, fcol]
    piece[...] = final.astype(BF16)

    ci = send([remote(piece, piece, c_s.at[d], c_r.at[d], peer) for d, _, _, peer in a_peers])
    for c in ci:
        c.wait_recv()

    for c in sent:
        c.wait_send()
    for j in range(8):
        zt = 2 * j + zhi
        copy = remote(ws.at[j], wr.at[zlo], ws_s.at[j], ws_r.at[zlo], (at(y, zt), q))

        @pl.when(zt != z)
        def _():
            copy.wait_send()


def step(q, nk, nv, kc, vc, cache_len, resid, gain, w_gate, w_up, w_down):
    hbm = pl.BlockSpec(memory_space=pl.ANY)
    dma = lambda n: pltpu.SemaphoreType.DMA((n,))
    vm = pltpu.VMEM
    sems = []
    for n in (8, 16, 4, 16, 16, 8, 8, 16, 4):
        sems += [dma(n), dma(n)]
    return pl.pallas_call(
        kernel,
        out_shape=jax.ShapeDtypeStruct((4, 8, 2048), BF16),
        in_specs=[hbm] * 5 + [pl.BlockSpec(memory_space=pltpu.SMEM)] + [hbm] * 5,
        out_specs=pl.BlockSpec(memory_space=pltpu.VMEM),
        scratch_shapes=[
            vm((4, 8, 2048), BF16), vm((4, 8, 128), BF16), vm((4, 8, 128), BF16),
            vm((8, 32, 1024), BF16), vm((8, 32, 1024), BF16), vm((2, 8, 256), BF16), vm((2048,), BF16),
            vm((32, 768), BF16), vm((32, 768), BF16), vm((32, 768), BF16),
            vm((8, 32, 384), BF16), vm((8, 32, 384), BF16),
            vm((8, 2, 5, 8, 128), BF16), vm((16, 5, 8, 128), BF16),
            vm((5, 8, 128), BF16), vm((4, 5, 8, 128), BF16),
            vm((8, 4, 8, 256), BF16),
            vm((8, 32, 256), BF16), vm((8, 32, 256), BF16),
            vm((8, 32, 128), BF16),
            vm((8, 2, 16, 256), BF16), vm((16, 16, 256), BF16),
            vm((16, 256), BF16), vm((4, 16, 256), BF16),
            dma(10),
        ] + sems,
        compiler_params=pltpu.CompilerParams(
            collective_id=0, has_side_effects=True, vmem_limit_bytes=60 * 1024 * 1024
        ),
    )(q, nk, nv, kc, vc, cache_len, resid, gain, w_gate, w_up, w_down.T)


def solution(mesh):
    placed = (
        P(None, "req", None),
        P(None, "req", None),
        P(None, "req", None),
        P("req", "seq", None),
        P("req", "seq", None),
        P("req"),
        P(None, "req", None),
        P(),
        P("seq", "req"),
        P("seq", "req"),
        P("req", "seq"),
    )
    return jax.shard_map(step, mesh=mesh, in_specs=placed, out_specs=P(None, "req", None), check_vma=False)
```

```python
import functools
import math

import jax
import jax.numpy as jnp
from jax import lax
from jax.experimental import pallas as pl
from jax.experimental.pallas import tpu as pltpu
from jax.sharding import PartitionSpec as P

NEG_FILL = -1e30
EPSILON = 1e-06
F32 = jnp.float32
BF16 = jnp.bfloat16
NT = (((1,), (1,)), ((), ()))
SCALE = 1.0 / math.sqrt(128)


def split3(x):
    hi = x.astype(BF16).astype(F32)
    rest = x - hi
    mid = rest.astype(BF16).astype(F32)
    low = (rest - mid).astype(BF16).astype(F32)
    return (hi + pltpu.roll(mid, 16, 1) + pltpu.roll(low, 32, 1)).astype(BF16)


def join3(x):
    return x + pltpu.roll(x, 112, 1) + pltpu.roll(x, 96, 1)


def kernel(
    q_h, nk_h, nv_h, k_h, v_h, len_s, resid_h, gain_h, wg_h, wu_h, wd_h,
    out,
    q_v, nk_v, nv_v, k_v, v_v, res_v, gain_v, wg_v, wu_v, wd_v,
    ws, wr, us, ur, pa, ra, pb, rb, x_v, pp, rp, hh, dd, rd, ee, re,
    lsem,
    ws_s, ws_r, us_s, us_r, a_s, a_r, b_s, b_r, c_s, c_r, d_s, d_r, e_s, e_r, f_s, f_r, g_s, g_r, h_s, h_r,
):
    s = lax.axis_index("seq")
    q = lax.axis_index("req")
    y = lax.div(s, 16)
    z = lax.rem(s, 16)
    kb = lax.rem(z, 2)
    k = y * 2 + kb
    zpair = z + 1 - 2 * kb
    zh = lax.div(z, 4)
    zl = lax.rem(z, 4)
    half = lax.div(zl, 2)
    zhi = lax.div(z, 8)
    zlo = lax.rem(z, 8)

    def at(yy, zz):
        return yy * 16 + zz

    a_peers = []
    for dy in range(4):
        for dz in range(4):
            if dy or dz:
                yt, zt = lax.rem(y + dy, 4), lax.rem(zl + dz, 4)
                kt, ht = yt * 2 + lax.rem(zt, 2), lax.div(zt, 2)
                a_peers.append((4 * dy + dz, kt, ht, (at(yt, 4 * zh + zt), q)))
    a_peers.sort(key=lambda p: -(min(p[0] // 4, 4 - p[0] // 4) * 2 + min(p[0] % 4, 2)))
    z_peers = [(d, (at(y, lax.rem(z + 4 * d, 16)), q)) for d in (2, 1, 3)]
    c_peers = []
    for dq in range(8):
        for dh in range(2):
            if dq or dh:
                qt = lax.rem(q + dq, 8)
                ht = 1 - half if dh else half
                c_peers.append((2 * dq + dh, qt, ht, (at(y, 4 * zh + 2 * ht + kb), qt)))
    c_peers.sort(key=lambda p: -(min(p[0] // 4, 4 - p[0] // 4) + 2 * (p[0] % 2)))
    k_peers = []
    for dy in range(4):
        for dk in range(2):
            if dy or dk:
                yt = lax.rem(y + dy, 4)
                kt = yt * 2 + (1 - kb if dk else kb)
                k_peers.append((2 * dy + dk, kt, (at(yt, zpair if dk else z), q)))
    k_peers.sort(key=lambda p: -(min(p[0] // 2, 4 - p[0] // 2) + p[0] % 2))
    rest = [(at(y, 4 * lax.rem(zh + i, 4) + lax.rem(zl + j, 4)), q) for i in range(1, 4) for j in range(1, 4)]

    kcol = pl.ds(pl.multiple_of(k * 128, 128), 128)
    fcol = pl.ds(pl.multiple_of(k * 256, 256), 256)
    loads = [
        (wg_h, wg_v), (wu_h, wu_v), (wd_h, wd_v), (q_h, q_v), (k_h, k_v), (v_h, v_v),
        (nk_h.at[:, :, kcol], nk_v), (nv_h.at[:, :, kcol], nv_v),
        (resid_h.at[pl.ds(2 * half, 2), :, fcol], res_v), (gain_h, gain_v),
    ]
    loads = [pltpu.make_async_copy(a, b, lsem.at[i]) for i, (a, b) in enumerate(loads)]
    for c in loads:
        c.start()

    barrier = pltpu.get_barrier_semaphore()
    same = [p for p in c_peers if p[0] == 1][0]
    greeted = [p[-1] for p in a_peers + z_peers + c_peers if p is not same] + rest
    for peer in greeted:
        pl.semaphore_signal(barrier, inc=1, device_id=peer, device_id_type=pl.DeviceIdType.MESH)

    def remote(src, dst, ssem, rsem, peer):
        return pltpu.make_async_remote_copy(
            src_ref=src, dst_ref=dst, send_sem=ssem, recv_sem=rsem,
            device_id=peer, device_id_type=pl.DeviceIdType.MESH,
        )

    sent = []

    def send(copies):
        for c in copies:
            c.start()
        sent.extend(copies)
        return copies

    for c in loads[3:6]:
        c.wait()
    row = lax.broadcasted_iota(jnp.int32, (64, 256), 0) & 7
    col = lax.broadcasted_iota(jnp.int32, (64, 256), 1)
    limit = jnp.zeros((64, 256), jnp.int32)
    for r in range(8):
        limit = jnp.where(row == r, len_s[r], limit)
    mask = (lax.shift_right_logical(col, 5) == row) & ((col & 31) + s * 32 < limit)
    lane = lax.broadcasted_iota(jnp.int32, (8, 128), 1)

    def stats(top, tot):
        tile = jnp.zeros((8, 128), F32)
        for i in range(4):
            tile = jnp.where(lane == i, top[8 * i:8 * i + 8], tile)
            tile = jnp.where(lane == 48 + i, tot[8 * i:8 * i + 8], tile)
        return tile

    for kv in range(8):
        qk = jnp.concatenate(
            [
                q_v[tt, :, 128 * (2 * kv + gg):128 * (2 * kv + gg) + 128].astype(F32)
                for tt in range(4) for gg in range(2)
            ],
            axis=0,
        ).astype(BF16)
        keys = k_v[:, :, 128 * kv:128 * kv + 128].reshape(256, 128)
        vals = v_v[:, :, 128 * kv:128 * kv + 128].reshape(256, 128)
        sc = lax.dot_general(qk, keys, NT, preferred_element_type=F32) * SCALE
        sc = jnp.where(mask, sc, NEG_FILL)
        top = jnp.max(sc, axis=1, keepdims=True)
        w = jnp.where(mask, jnp.exp(sc - top), 0.0).astype(BF16)
        tot = jnp.sum(w.astype(F32), axis=1, keepdims=True)
        acc = jnp.dot(w, vals, preferred_element_type=F32).astype(BF16)
        for h in range(2):
            pa[kv, h, 0:4] = acc[32 * h:32 * h + 32].reshape(4, 8, 128)
            pa[kv, h, 4] = split3(stats(top[32 * h:32 * h + 32], tot[32 * h:32 * h + 32]))

    pl.semaphore_wait(barrier, len(greeted))

    ca = send([remote(pa.at[kt, ht], ra.at[d], a_s.at[d], a_r.at[d], peer) for d, kt, ht, peer in a_peers])

    for c in loads[:3]:
        c.wait()
    whole = [wg_v[...].astype(F32), wu_v[...].astype(F32), wd_v[...].astype(F32)]
    keep = lax.broadcasted_iota(jnp.int32, (32, 128), 1) < 96
    for j in range(8):
        base, off = (96 * j) // 128 * 128, (96 * j) % 128
        for i, w in enumerate(whole):
            if off + 96 <= 128:
                piece = w[:, base:base + 128]
                if off:
                    piece = pltpu.roll(piece, 128 - off, 1)
            else:
                piece = pltpu.roll(w[:, base:base + 256], 256 - off, 1)[:, :128]
            part = jnp.where(keep, piece, 0.0).astype(BF16)
            if i < 2:
                ws[j, :, 128 * i:128 * i + 128] = part
            else:
                us[j] = part

    def weights(src, dst, ssem, rsem, action):
        for j in range(8):
            zt = 2 * j + zhi
            copy = remote(src.at[j], dst.at[zlo], ssem.at[j], rsem.at[zlo], (at(y, zt), q))
            if action == "wait":
                copy = remote(src.at[j], dst.at[j], ssem.at[j], rsem.at[j], (s, q))

            @pl.when(8 * kb + j != z if action == "wait" else zt != z)
            def _():
                {"start": copy.start, "wait": copy.wait_recv, "end": copy.wait_send}[action]()

            if action == "start":

                @pl.when(zt == z)
                def _():
                    dst[zlo] = src[j]

    gate_up = (ws, wr, ws_s, ws_r)
    down_w = (us, ur, us_s, us_r)

    for c in loads[6:]:
        c.wait()
    qf = jnp.concatenate(
        [
            q_v[2 * half + tt, :, pl.ds(pl.multiple_of(k * 256 + 128 * gg, 128), 128)].astype(F32)
            for tt in range(2) for gg in range(2)
        ],
        axis=0,
    ).astype(BF16)
    nk = nk_v[...].astype(F32).reshape(32, 128).astype(BF16)
    nv = nv_v[...].astype(F32).reshape(32, 128).astype(BF16)
    fs = lax.dot_general(qf, nk, NT, preferred_element_type=F32) * SCALE
    frow = lax.broadcasted_iota(jnp.int32, (32, 32), 0)
    fcl = lax.broadcasted_iota(jnp.int32, (32, 32), 1)
    fmask = ((fcl & 7) == (frow & 7)) & (lax.shift_right_logical(fcl, 3) <= lax.shift_right_logical(frow, 4) + 2 * half)
    fs = jnp.where(fmask, fs, NEG_FILL)
    ftop = jnp.max(fs, axis=1, keepdims=True)
    fw = jnp.where(fmask, jnp.exp(fs - ftop), 0.0).astype(BF16)
    ftot = jnp.sum(fw.astype(F32), axis=1, keepdims=True)
    facc = jnp.dot(fw, nv, preferred_element_type=F32)
    fstat = stats(ftop, ftot)

    def merge(parts):
        peak = functools.reduce(jnp.maximum, parts)
        fac = [jnp.exp(v - peak) for v in parts]
        total = sum(pltpu.roll(f, 48, 1) * v for f, v in zip(fac, parts))
        return peak, fac, total

    ra[0] = pa[k, half]
    for c in ca:
        c.wait_recv()
    peak, fac, total = merge([join3(ra[d, 4].astype(F32)) for d in range(16)])
    for i in range(4):
        pb[i] = sum(fac[d][:, i:i + 1] * ra[d, i].astype(F32) for d in range(16)).astype(BF16)
    pb[4] = split3(jnp.where(lane < 4, peak, jnp.where((lane >= 48) & (lane < 52), total, 0.0)))

    cb = send([remote(pb, rb.at[zh], b_s.at[d], b_r.at[d], peer) for d, peer in z_peers])
    weights(*gate_up, "start")
    rb[zh] = pb[...]
    for c in cb:
        c.wait_recv()
    _, fac, total = merge([join3(rb[d, 4].astype(F32)) for d in range(4)] + [fstat])
    inverse = pltpu.roll(total, 80, 1)
    for i in range(4):
        acc = sum(fac[d][:, i:i + 1] * rb[d, i].astype(F32) for d in range(4))
        acc = acc + fac[4][:, i:i + 1] * facc[8 * i:8 * i + 8]
        attn = (acc / inverse[:, i:i + 1]).astype(BF16).astype(F32)
        tt, gg = i // 2, i % 2
        x_v[q, 2 * half + tt, :, 128 * gg:128 * gg + 128] = (
            res_v[tt, :, 128 * gg:128 * gg + 128].astype(F32) + attn
        ).astype(BF16)

    mine = x_v.at[q, pl.ds(2 * half, 2)]
    cd = send([remote(mine, mine, d_s.at[d], d_r.at[d], peer) for d, _, _, peer in c_peers])
    weights(*down_w, "start")
    for c in cd:
        c.wait_recv()
    weights(*gate_up, "wait")

    xf = x_v[...].astype(F32).reshape(256, 256)
    square = jnp.sum(xf * xf, axis=1, keepdims=True)
    xg = (xf * gain_v[fcol].astype(F32).reshape(1, 256)).astype(BF16)
    gu = jnp.dot(xg, wr[...].reshape(256, 256), preferred_element_type=F32)
    hi = square.astype(BF16).astype(F32)
    lane2 = lax.broadcasted_iota(jnp.int32, (256, 256), 1)
    gu = jnp.where(lane2 == 96, hi, jnp.where(lane2 == 97, square - hi, gu))
    pp[...] = gu.astype(BF16).reshape(8, 32, 256)
    ce = send([remote(pp.at[kt], rp.at[d], e_s.at[d], e_r.at[d], peer) for d, kt, peer in k_peers])
    rp[0] = pp[k]
    for c in ce:
        c.wait_recv()
    gu = jnp.sum(rp[...].astype(F32), axis=0)
    lane32 = lax.broadcasted_iota(jnp.int32, (32, 128), 1)
    gate, up = gu[:, :128], gu[:, 128:]
    square = jnp.sum(jnp.where((lane32 == 96) | (lane32 == 97), gate, 0.0), axis=1, keepdims=True)
    norm = lax.rsqrt(square * (1.0 / 2048) + EPSILON)
    gate = gate * norm
    up = up * norm
    hidden = gate / (1.0 + jnp.exp(-gate)) * up
    hh[k] = jnp.where(lane32 < 96, hidden, 0.0).astype(BF16)
    cf = send([remote(hh.at[k], hh.at[k], f_s.at[d], f_r.at[d], peer) for d, _, peer in k_peers])
    for c in cf:
        c.wait_recv()

    weights(*down_w, "wait")
    down = lax.dot_general(
        hh[...].reshape(256, 128), ur[...].reshape(256, 128), NT, preferred_element_type=F32
    )
    dd[...] = down.astype(BF16).reshape(8, 2, 16, 256)
    cg = send([remote(dd.at[qt, ht], rd.at[d], g_s.at[d], g_r.at[d], peer) for d, qt, ht, peer in c_peers])
    rd[0] = dd[q, half]
    for c in cg:
        c.wait_recv()
    ee[...] = jnp.sum(rd[...].astype(F32), axis=0).astype(BF16)
    ch = send([remote(ee, re.at[zh], h_s.at[d], h_r.at[d], peer) for d, peer in z_peers])
    re[zh] = ee[...]
    for c in ch:
        c.wait_recv()
    final = mine[...].astype(F32) + jnp.sum(re[...].astype(F32), axis=0).reshape(2, 8, 256)
    piece = out.at[pl.ds(2 * half, 2), :, fcol]
    piece[...] = final.astype(BF16)

    ci = send([remote(piece, piece, c_s.at[d], c_r.at[d], peer) for d, _, _, peer in a_peers])
    for c in ci:
        c.wait_recv()

    for c in sent:
        c.wait_send()
    weights(*gate_up, "end")
    weights(*down_w, "end")


def step(q, nk, nv, kc, vc, cache_len, resid, gain, w_gate, w_up, w_down):
    hbm = pl.BlockSpec(memory_space=pl.ANY)
    dma = lambda n: pltpu.SemaphoreType.DMA((n,))
    vm = pltpu.VMEM
    sems = []
    for n in (8, 8, 16, 4, 16, 16, 8, 8, 16, 4):
        sems += [dma(n), dma(n)]
    return pl.pallas_call(
        kernel,
        out_shape=jax.ShapeDtypeStruct((4, 8, 2048), BF16),
        in_specs=[hbm] * 5 + [pl.BlockSpec(memory_space=pltpu.SMEM)] + [hbm] * 5,
        out_specs=pl.BlockSpec(memory_space=pltpu.VMEM),
        scratch_shapes=[
            vm((4, 8, 2048), BF16), vm((4, 8, 128), BF16), vm((4, 8, 128), BF16),
            vm((8, 32, 1024), BF16), vm((8, 32, 1024), BF16), vm((2, 8, 256), BF16), vm((2048,), BF16),
            vm((32, 768), BF16), vm((32, 768), BF16), vm((32, 768), BF16),
            vm((8, 32, 256), BF16), vm((8, 32, 256), BF16), vm((8, 32, 128), BF16), vm((8, 32, 128), BF16),
            vm((8, 2, 5, 8, 128), BF16), vm((16, 5, 8, 128), BF16),
            vm((5, 8, 128), BF16), vm((4, 5, 8, 128), BF16),
            vm((8, 4, 8, 256), BF16),
            vm((8, 32, 256), BF16), vm((8, 32, 256), BF16),
            vm((8, 32, 128), BF16),
            vm((8, 2, 16, 256), BF16), vm((16, 16, 256), BF16),
            vm((16, 256), BF16), vm((4, 16, 256), BF16),
            dma(10),
        ] + sems,
        compiler_params=pltpu.CompilerParams(
            collective_id=0, has_side_effects=True, vmem_limit_bytes=60 * 1024 * 1024
        ),
    )(q, nk, nv, kc, vc, cache_len, resid, gain, w_gate, w_up, w_down.T)


def solution(mesh):
    placed = (
        P(None, "req", None),
        P(None, "req", None),
        P(None, "req", None),
        P("req", "seq", None),
        P("req", "seq", None),
        P("req"),
        P(None, "req", None),
        P(),
        P("seq", "req"),
        P("seq", "req"),
        P("req", "seq"),
    )
    return jax.shard_map(step, mesh=mesh, in_specs=placed, out_specs=P(None, "req", None), check_vma=False)
```

```python
import functools
import math

import jax
import jax.numpy as jnp
from jax import lax
from jax.experimental import pallas as pl
from jax.experimental.pallas import tpu as pltpu
from jax.sharding import PartitionSpec as P

NEG_FILL = -1e30
EPSILON = 1e-06
F32 = jnp.float32
BF16 = jnp.bfloat16
NT = (((1,), (1,)), ((), ()))
SCALE = 1.0 / math.sqrt(128)


def split3(x):
    hi = x.astype(BF16).astype(F32)
    rest = x - hi
    mid = rest.astype(BF16).astype(F32)
    low = (rest - mid).astype(BF16).astype(F32)
    return (hi + pltpu.roll(mid, 16, 1) + pltpu.roll(low, 32, 1)).astype(BF16)


def join3(x):
    return x + pltpu.roll(x, 112, 1) + pltpu.roll(x, 96, 1)


def kernel(
    q_h, nk_h, nv_h, k_h, v_h, len_s, resid_h, gain_h, wg_h, wu_h, wd_h,
    out,
    q_v, nk_v, nv_v, k_v, v_v, res_v, gain_v, wg_v, wu_v, wd_v,
    ws, wr, us, ur, pa, ra, pb, rb, x_v, pp, rp, hh, dd, rd, ee, re,
    lsem,
    ws_s, ws_r, us_s, us_r, a_s, a_r, b_s, b_r, c_s, c_r, d_s, d_r, e_s, e_r, f_s, f_r, g_s, g_r, h_s, h_r,
):
    s = lax.axis_index("seq")
    q = lax.axis_index("req")
    y = lax.div(s, 16)
    z = lax.rem(s, 16)
    kb = lax.rem(z, 2)
    k = y * 2 + kb
    zpair = z + 1 - 2 * kb
    zh = lax.div(z, 4)
    zl = lax.rem(z, 4)
    half = lax.div(zl, 2)
    zhi = lax.div(z, 8)
    zlo = lax.rem(z, 8)

    def at(yy, zz):
        return yy * 16 + zz

    a_peers = []
    for dy in range(4):
        for dz in range(4):
            if dy or dz:
                yt, zt = lax.rem(y + dy, 4), lax.rem(zl + dz, 4)
                kt, ht = yt * 2 + lax.rem(zt, 2), lax.div(zt, 2)
                a_peers.append((4 * dy + dz, kt, ht, (at(yt, 4 * zh + zt), q)))
    a_peers.sort(key=lambda p: -(min(p[0] // 4, 4 - p[0] // 4) * 2 + min(p[0] % 4, 2)))
    z_peers = [(d, (at(y, lax.rem(z + 4 * d, 16)), q)) for d in (2, 1, 3)]
    c_peers = []
    for dq in range(8):
        for dh in range(2):
            if dq or dh:
                qt = lax.rem(q + dq, 8)
                ht = 1 - half if dh else half
                c_peers.append((2 * dq + dh, qt, ht, (at(y, 4 * zh + 2 * ht + kb), qt)))
    c_peers.sort(key=lambda p: -(min(p[0] // 4, 4 - p[0] // 4) + 2 * (p[0] % 2)))
    k_peers = []
    for dy in range(4):
        for dk in range(2):
            if dy or dk:
                yt = lax.rem(y + dy, 4)
                kt = yt * 2 + (1 - kb if dk else kb)
                k_peers.append((2 * dy + dk, kt, (at(yt, zpair if dk else z), q)))
    k_peers.sort(key=lambda p: -(min(p[0] // 2, 4 - p[0] // 2) + p[0] % 2))
    rest = [(at(y, 4 * lax.rem(zh + i, 4) + lax.rem(zl + j, 4)), q) for i in range(1, 4) for j in range(1, 4)]

    kcol = pl.ds(pl.multiple_of(k * 128, 128), 128)
    fcol = pl.ds(pl.multiple_of(k * 256, 256), 256)
    loads = [
        (wg_h, wg_v), (wu_h, wu_v), (wd_h, wd_v), (q_h, q_v), (k_h, k_v), (v_h, v_v),
        (nk_h.at[:, :, kcol], nk_v), (nv_h.at[:, :, kcol], nv_v),
        (resid_h.at[pl.ds(2 * half, 2), :, fcol], res_v), (gain_h, gain_v),
    ]
    loads = [pltpu.make_async_copy(a, b, lsem.at[i]) for i, (a, b) in enumerate(loads)]
    for c in loads:
        c.start()

    barrier = pltpu.get_barrier_semaphore()
    same = [p for p in c_peers if p[0] == 1][0]
    greeted = [p[-1] for p in a_peers + z_peers + c_peers if p is not same] + rest
    for peer in greeted:
        pl.semaphore_signal(barrier, inc=1, device_id=peer, device_id_type=pl.DeviceIdType.MESH)

    def remote(src, dst, ssem, rsem, peer):
        return pltpu.make_async_remote_copy(
            src_ref=src, dst_ref=dst, send_sem=ssem, recv_sem=rsem,
            device_id=peer, device_id_type=pl.DeviceIdType.MESH,
        )

    sent = []

    def send(copies):
        for c in copies:
            c.start()
        sent.extend(copies)
        return copies

    for c in loads[3:6]:
        c.wait()
    row = lax.broadcasted_iota(jnp.int32, (64, 256), 0) & 7
    col = lax.broadcasted_iota(jnp.int32, (64, 256), 1)
    limit = jnp.zeros((64, 256), jnp.int32)
    for r in range(8):
        limit = jnp.where(row == r, len_s[r], limit)
    mask = (lax.shift_right_logical(col, 5) == row) & ((col & 31) + s * 32 < limit)
    lane = lax.broadcasted_iota(jnp.int32, (8, 128), 1)

    def stats(top, tot):
        tile = jnp.zeros((8, 128), F32)
        for i in range(4):
            tile = jnp.where(lane == i, top[8 * i:8 * i + 8], tile)
            tile = jnp.where(lane == 48 + i, tot[8 * i:8 * i + 8], tile)
        return tile

    for kv in range(8):
        qk = jnp.concatenate(
            [
                q_v[tt, :, 128 * (2 * kv + gg):128 * (2 * kv + gg) + 128].astype(F32)
                for tt in range(4) for gg in range(2)
            ],
            axis=0,
        ).astype(BF16)
        keys = k_v[:, :, 128 * kv:128 * kv + 128].reshape(256, 128)
        vals = v_v[:, :, 128 * kv:128 * kv + 128].reshape(256, 128)
        sc = lax.dot_general(qk, keys, NT, preferred_element_type=F32) * SCALE
        sc = jnp.where(mask, sc, NEG_FILL)
        top = jnp.max(sc, axis=1, keepdims=True)
        w = jnp.where(mask, jnp.exp(sc - top), 0.0).astype(BF16)
        tot = jnp.sum(w.astype(F32), axis=1, keepdims=True)
        acc = jnp.dot(w, vals, preferred_element_type=F32).astype(BF16)
        for h in range(2):
            pa[kv, h, 0:4] = acc[32 * h:32 * h + 32].reshape(4, 8, 128)
            pa[kv, h, 4] = split3(stats(top[32 * h:32 * h + 32], tot[32 * h:32 * h + 32]))

    pl.semaphore_wait(barrier, len(greeted))

    ca = send([remote(pa.at[kt, ht], ra.at[d], a_s.at[d], a_r.at[d], peer) for d, kt, ht, peer in a_peers])

    for c in loads[:3]:
        c.wait()
    whole = [wg_v[...].astype(F32), wu_v[...].astype(F32), wd_v[...].astype(F32)]
    keep = lax.broadcasted_iota(jnp.int32, (32, 128), 1) < 96
    for j in range(8):
        base, off = (96 * j) // 128 * 128, (96 * j) % 128
        for i, w in enumerate(whole):
            if off + 96 <= 128:
                piece = w[:, base:base + 128]
                if off:
                    piece = pltpu.roll(piece, 128 - off, 1)
            else:
                piece = pltpu.roll(w[:, base:base + 256], 256 - off, 1)[:, :128]
            part = jnp.where(keep, piece, 0.0).astype(BF16)
            if i < 2:
                ws[j, :, 128 * i:128 * i + 128] = part
            else:
                us[j] = part

    def weights(src, dst, ssem, rsem, action):
        for j in range(8):
            zt = 2 * j + zhi
            copy = remote(src.at[j], dst.at[zlo], ssem.at[j], rsem.at[zlo], (at(y, zt), q))
            if action == "wait":
                copy = remote(src.at[j], dst.at[j], ssem.at[j], rsem.at[j], (s, q))

            @pl.when(8 * kb + j != z if action == "wait" else zt != z)
            def _():
                {"start": copy.start, "wait": copy.wait_recv, "end": copy.wait_send}[action]()

            if action == "start":

                @pl.when(zt == z)
                def _():
                    dst[zlo] = src[j]

    gate_up = (ws, wr, ws_s, ws_r)
    down_w = (us, ur, us_s, us_r)

    for c in loads[6:]:
        c.wait()
    qf = jnp.concatenate(
        [
            q_v[2 * half + tt, :, pl.ds(pl.multiple_of(k * 256 + 128 * gg, 128), 128)].astype(F32)
            for tt in range(2) for gg in range(2)
        ],
        axis=0,
    ).astype(BF16)
    nk = nk_v[...].astype(F32).reshape(32, 128).astype(BF16)
    nv = nv_v[...].astype(F32).reshape(32, 128).astype(BF16)
    fs = lax.dot_general(qf, nk, NT, preferred_element_type=F32) * SCALE
    frow = lax.broadcasted_iota(jnp.int32, (32, 32), 0)
    fcl = lax.broadcasted_iota(jnp.int32, (32, 32), 1)
    fmask = ((fcl & 7) == (frow & 7)) & (lax.shift_right_logical(fcl, 3) <= lax.shift_right_logical(frow, 4) + 2 * half)
    fs = jnp.where(fmask, fs, NEG_FILL)
    ftop = jnp.max(fs, axis=1, keepdims=True)
    fw = jnp.where(fmask, jnp.exp(fs - ftop), 0.0).astype(BF16)
    ftot = jnp.sum(fw.astype(F32), axis=1, keepdims=True)
    facc = jnp.dot(fw, nv, preferred_element_type=F32)
    fstat = stats(ftop, ftot)

    def merge(parts):
        peak = functools.reduce(jnp.maximum, parts)
        fac = [jnp.exp(v - peak) for v in parts]
        total = sum(pltpu.roll(f, 48, 1) * v for f, v in zip(fac, parts))
        return peak, fac, total

    ra[0] = pa[k, half]
    for c in ca:
        c.wait_recv()
    peak, fac, total = merge([join3(ra[d, 4].astype(F32)) for d in range(16)])
    for i in range(4):
        pb[i] = sum(fac[d][:, i:i + 1] * ra[d, i].astype(F32) for d in range(16)).astype(BF16)
    pb[4] = split3(jnp.where(lane < 4, peak, jnp.where((lane >= 48) & (lane < 52), total, 0.0)))

    cb = send([remote(pb, rb.at[zh], b_s.at[d], b_r.at[d], peer) for d, peer in z_peers])
    weights(*gate_up, "start")
    rb[zh] = pb[...]
    for c in cb:
        c.wait_recv()
    _, fac, total = merge([join3(rb[d, 4].astype(F32)) for d in range(4)] + [fstat])
    inverse = pltpu.roll(total, 80, 1)
    for i in range(4):
        acc = sum(fac[d][:, i:i + 1] * rb[d, i].astype(F32) for d in range(4))
        acc = acc + fac[4][:, i:i + 1] * facc[8 * i:8 * i + 8]
        attn = (acc / inverse[:, i:i + 1]).astype(BF16).astype(F32)
        tt, gg = i // 2, i % 2
        x_v[q, 2 * half + tt, :, 128 * gg:128 * gg + 128] = (
            res_v[tt, :, 128 * gg:128 * gg + 128].astype(F32) + attn
        ).astype(BF16)

    mine = x_v.at[q, pl.ds(2 * half, 2)]
    cd = send([remote(mine, mine, d_s.at[d], d_r.at[d], peer) for d, _, _, peer in c_peers])
    weights(*down_w, "start")
    for c in cd:
        c.wait_recv()
    weights(*gate_up, "wait")

    xf = x_v[...].astype(F32).reshape(256, 256)
    square = jnp.sum(xf * xf, axis=1, keepdims=True)
    xg = (xf * gain_v[fcol].astype(F32).reshape(1, 256)).astype(BF16)
    gu = jnp.dot(xg, wr[...].reshape(256, 256), preferred_element_type=F32)
    hi = square.astype(BF16).astype(F32)
    lane2 = lax.broadcasted_iota(jnp.int32, (256, 256), 1)
    gu = jnp.where(lane2 == 96, hi, jnp.where(lane2 == 97, square - hi, gu))
    pp[...] = gu.astype(BF16).reshape(8, 32, 256)
    ce = send([remote(pp.at[kt], rp.at[d], e_s.at[d], e_r.at[d], peer) for d, kt, peer in k_peers])
    rp[0] = pp[k]
    for c in ce:
        c.wait_recv()
    gu = jnp.sum(rp[...].astype(F32), axis=0)
    lane32 = lax.broadcasted_iota(jnp.int32, (32, 128), 1)
    gate, up = gu[:, :128], gu[:, 128:]
    square = jnp.sum(jnp.where((lane32 == 96) | (lane32 == 97), gate, 0.0), axis=1, keepdims=True)
    norm = lax.rsqrt(square * (1.0 / 2048) + EPSILON)
    gate = gate * norm
    up = up * norm
    hidden = gate / (1.0 + jnp.exp(-gate)) * up
    hh[k] = jnp.where(lane32 < 96, hidden, 0.0).astype(BF16)
    cf = send([remote(hh.at[k], hh.at[k], f_s.at[d], f_r.at[d], peer) for d, _, peer in k_peers])
    for c in cf:
        c.wait_recv()

    weights(*down_w, "wait")
    down = lax.dot_general(
        hh[...].reshape(256, 128), ur[...].reshape(256, 128), NT, preferred_element_type=F32
    )
    dd[...] = down.astype(BF16).reshape(8, 2, 16, 256)
    cg = send([remote(dd.at[qt, ht], rd.at[d], g_s.at[d], g_r.at[d], peer) for d, qt, ht, peer in c_peers])
    rd[0] = dd[q, half]
    for c in cg:
        c.wait_recv()
    ee[...] = jnp.sum(rd[...].astype(F32), axis=0).astype(BF16)
    ch = send([remote(ee, re.at[zh], h_s.at[d], h_r.at[d], peer) for d, peer in z_peers])
    re[zh] = ee[...]
    for c in ch:
        c.wait_recv()
    final = mine[...].astype(F32) + jnp.sum(re[...].astype(F32), axis=0).reshape(2, 8, 256)
    piece = out.at[pl.ds(2 * half, 2), :, fcol]
    piece[...] = final.astype(BF16)

    ci = send([remote(piece, piece, c_s.at[d], c_r.at[d], peer) for d, _, _, peer in a_peers])
    for c in ci:
        c.wait_recv()

    for c in sent:
        c.wait_send()
    weights(*gate_up, "end")
    weights(*down_w, "end")


def step(q, nk, nv, kc, vc, cache_len, resid, gain, w_gate, w_up, w_down):
    hbm = pl.BlockSpec(memory_space=pl.ANY)
    dma = lambda n: pltpu.SemaphoreType.DMA((n,))
    vm = pltpu.VMEM
    sems = []
    for n in (8, 8, 16, 4, 16, 16, 8, 8, 16, 4):
        sems += [dma(n), dma(n)]
    return pl.pallas_call(
        kernel,
        out_shape=jax.ShapeDtypeStruct((4, 8, 2048), BF16),
        in_specs=[hbm] * 5 + [pl.BlockSpec(memory_space=pltpu.SMEM)] + [hbm] * 5,
        out_specs=pl.BlockSpec(memory_space=pltpu.VMEM),
        scratch_shapes=[
            vm((4, 8, 2048), BF16), vm((4, 8, 128), BF16), vm((4, 8, 128), BF16),
            vm((8, 32, 1024), BF16), vm((8, 32, 1024), BF16), vm((2, 8, 256), BF16), vm((2048,), BF16),
            vm((32, 768), BF16), vm((32, 768), BF16), vm((32, 768), BF16),
            vm((8, 32, 256), BF16), vm((8, 32, 256), BF16), vm((8, 32, 128), BF16), vm((8, 32, 128), BF16),
            vm((8, 2, 5, 8, 128), BF16), vm((16, 5, 8, 128), BF16),
            vm((5, 8, 128), BF16), vm((4, 5, 8, 128), BF16),
            vm((8, 4, 8, 256), BF16),
            vm((8, 32, 256), BF16), vm((8, 32, 256), BF16),
            vm((8, 32, 128), BF16),
            vm((8, 2, 16, 256), BF16), vm((16, 16, 256), BF16),
            vm((16, 256), BF16), vm((4, 16, 256), BF16),
            dma(10),
        ] + sems,
        compiler_params=pltpu.CompilerParams(
            collective_id=0, has_side_effects=True, vmem_limit_bytes=16 * 1024 * 1024
        ),
    )(*[pltpu.with_memory_space_constraint(a, pltpu.HBM) for a in (q, nk, nv, kc, vc, cache_len, resid, gain, w_gate, w_up, w_down.T)])


def solution(mesh):
    placed = (
        P(None, "req", None),
        P(None, "req", None),
        P(None, "req", None),
        P("req", "seq", None),
        P("req", "seq", None),
        P("req"),
        P(None, "req", None),
        P(),
        P("seq", "req"),
        P("seq", "req"),
        P("req", "seq"),
    )
    return jax.shard_map(step, mesh=mesh, in_specs=placed, out_specs=P(None, "req", None), check_vma=False)
```

```python
import functools
import math

import jax
import jax.numpy as jnp
from jax import lax
from jax.experimental import pallas as pl
from jax.experimental.pallas import tpu as pltpu
from jax.sharding import PartitionSpec as P

NEG_FILL = -1e30
EPSILON = 1e-06
F32 = jnp.float32
BF16 = jnp.bfloat16
NT = (((1,), (1,)), ((), ()))
SCALE = 1.0 / math.sqrt(128)


def split3(x):
    hi = x.astype(BF16).astype(F32)
    rest = x - hi
    mid = rest.astype(BF16).astype(F32)
    low = (rest - mid).astype(BF16).astype(F32)
    return (hi + pltpu.roll(mid, 16, 1) + pltpu.roll(low, 32, 1)).astype(BF16)


def join3(x):
    return x + pltpu.roll(x, 112, 1) + pltpu.roll(x, 96, 1)


def kernel(
    q_h, nk_h, nv_h, k_h, v_h, len_s, resid_h, gain_h, wg_h, wu_h, wd_h,
    out,
    q_v, nk_v, nv_v, k_v, v_v, res_v, gain_v, wg_v, wu_v, wd_v,
    ws, wr, us, ur, pa, ra, pb, rb, x_v, pp, rp, hh, dd, rd, ee, re,
    lsem, near1, near2,
    ws_s, ws_r, us_s, us_r, a_s, a_r, b_s, b_r, c_s, c_r, d_s, d_r, e_s, e_r, f_s, f_r, g_s, g_r, h_s, h_r,
):
    s = lax.axis_index("seq")
    q = lax.axis_index("req")
    y = lax.div(s, 16)
    z = lax.rem(s, 16)
    kb = lax.rem(z, 2)
    k = y * 2 + kb
    zpair = z + 1 - 2 * kb
    zh = lax.div(z, 4)
    zl = lax.rem(z, 4)
    half = lax.div(zl, 2)
    zhi = lax.div(z, 8)
    zlo = lax.rem(z, 8)

    def at(yy, zz):
        return yy * 16 + zz

    a_peers = []
    for dy in range(4):
        for dz in range(4):
            if dy or dz:
                yt, zt = lax.rem(y + dy, 4), lax.rem(zl + dz, 4)
                kt, ht = yt * 2 + lax.rem(zt, 2), lax.div(zt, 2)
                a_peers.append((4 * dy + dz, kt, ht, (at(yt, 4 * zh + zt), q)))
    a_peers.sort(key=lambda p: -(min(p[0] // 4, 4 - p[0] // 4) * 2 + min(p[0] % 4, 2)))
    z_peers = [(d, (at(y, lax.rem(z + 4 * d, 16)), q)) for d in (2, 1, 3)]
    c_peers = []
    for dq in range(8):
        for dh in range(2):
            if dq or dh:
                qt = lax.rem(q + dq, 8)
                ht = 1 - half if dh else half
                c_peers.append((2 * dq + dh, qt, ht, (at(y, 4 * zh + 2 * ht + kb), qt)))
    c_peers.sort(key=lambda p: -(min(p[0] // 4, 4 - p[0] // 4) + 2 * (p[0] % 2)))
    k_peers = []
    for dy in range(4):
        for dk in range(2):
            if dy or dk:
                yt = lax.rem(y + dy, 4)
                kt = yt * 2 + (1 - kb if dk else kb)
                k_peers.append((2 * dy + dk, kt, (at(yt, zpair if dk else z), q)))
    k_peers.sort(key=lambda p: -(min(p[0] // 2, 4 - p[0] // 2) + p[0] % 2))
    steps_z = [p[-1] for p in z_peers if p[0] != 2]

    kcol = pl.ds(pl.multiple_of(k * 128, 128), 128)
    fcol = pl.ds(pl.multiple_of(k * 256, 256), 256)
    loads = [
        (wg_h, wg_v), (wu_h, wu_v), (wd_h, wd_v), (q_h, q_v), (k_h, k_v), (v_h, v_v),
        (nk_h.at[:, :, kcol], nk_v), (nv_h.at[:, :, kcol], nv_v),
        (resid_h.at[pl.ds(2 * half, 2), :, fcol], res_v), (gain_h, gain_v),
    ]
    loads = [pltpu.make_async_copy(a, b, lsem.at[i]) for i, (a, b) in enumerate(loads)]
    for c in loads:
        c.start()

    barrier = pltpu.get_barrier_semaphore()
    same = [p for p in c_peers if p[0] == 1][0]
    greeted = [p[-1] for p in a_peers + c_peers if p is not same] + steps_z
    for peer in greeted:
        pl.semaphore_signal(barrier, inc=1, device_id=peer, device_id_type=pl.DeviceIdType.MESH)

    def remote(src, dst, ssem, rsem, peer):
        return pltpu.make_async_remote_copy(
            src_ref=src, dst_ref=dst, send_sem=ssem, recv_sem=rsem,
            device_id=peer, device_id_type=pl.DeviceIdType.MESH,
        )

    def tell(sem):
        for peer in steps_z:
            pl.semaphore_signal(sem, inc=1, device_id=peer, device_id_type=pl.DeviceIdType.MESH)

    sent = []

    def send(copies):
        for c in copies:
            c.start()
        sent.extend(copies)
        return copies

    for c in loads[3:6]:
        c.wait()
    row = lax.broadcasted_iota(jnp.int32, (64, 256), 0) & 7
    col = lax.broadcasted_iota(jnp.int32, (64, 256), 1)
    limit = jnp.zeros((64, 256), jnp.int32)
    for r in range(8):
        limit = jnp.where(row == r, len_s[r], limit)
    mask = (lax.shift_right_logical(col, 5) == row) & ((col & 31) + s * 32 < limit)
    lane = lax.broadcasted_iota(jnp.int32, (8, 128), 1)

    def stats(top, tot):
        tile = jnp.zeros((8, 128), F32)
        for i in range(4):
            tile = jnp.where(lane == i, top[8 * i:8 * i + 8], tile)
            tile = jnp.where(lane == 48 + i, tot[8 * i:8 * i + 8], tile)
        return tile

    for kv in range(8):
        qk = jnp.concatenate(
            [
                q_v[tt, :, 128 * (2 * kv + gg):128 * (2 * kv + gg) + 128].astype(F32)
                for tt in range(4) for gg in range(2)
            ],
            axis=0,
        ).astype(BF16)
        keys = k_v[:, :, 128 * kv:128 * kv + 128].reshape(256, 128)
        vals = v_v[:, :, 128 * kv:128 * kv + 128].reshape(256, 128)
        sc = lax.dot_general(qk, keys, NT, preferred_element_type=F32) * SCALE
        sc = jnp.where(mask, sc, NEG_FILL)
        top = jnp.max(sc, axis=1, keepdims=True)
        w = jnp.where(mask, jnp.exp(sc - top), 0.0).astype(BF16)
        tot = jnp.sum(w.astype(F32), axis=1, keepdims=True)
        acc = jnp.dot(w, vals, preferred_element_type=F32).astype(BF16)
        for h in range(2):
            pa[kv, h, 0:4] = acc[32 * h:32 * h + 32].reshape(4, 8, 128)
            pa[kv, h, 4] = split3(stats(top[32 * h:32 * h + 32], tot[32 * h:32 * h + 32]))

    pl.semaphore_wait(barrier, len(greeted))

    ca = send([remote(pa.at[kt, ht], ra.at[d], a_s.at[d], a_r.at[d], peer) for d, kt, ht, peer in a_peers])

    tell(near1)

    for c in loads[:3]:
        c.wait()
    whole = [wg_v[...].astype(F32), wu_v[...].astype(F32), wd_v[...].astype(F32)]
    keep = lax.broadcasted_iota(jnp.int32, (32, 128), 1) < 96
    for j in range(8):
        base, off = (96 * j) // 128 * 128, (96 * j) % 128
        for i, w in enumerate(whole):
            if off + 96 <= 128:
                piece = w[:, base:base + 128]
                if off:
                    piece = pltpu.roll(piece, 128 - off, 1)
            else:
                piece = pltpu.roll(w[:, base:base + 256], 256 - off, 1)[:, :128]
            part = jnp.where(keep, piece, 0.0).astype(BF16)
            if i < 2:
                ws[j, :, 128 * i:128 * i + 128] = part
            else:
                us[j] = part

    def weights(src, dst, ssem, rsem, action):
        for j in range(8):
            block = lax.rem(lax.div(z, 2) + (4, 3, 5, 2, 6, 1, 7, 0)[j], 8)
            zt = 2 * block + zhi
            copy = remote(src.at[block], dst.at[zlo], ssem.at[j], rsem.at[zlo], (at(y, zt), q))
            if action == "wait":
                copy = remote(src.at[j], dst.at[j], ssem.at[j], rsem.at[j], (s, q))

            @pl.when(8 * kb + j != z if action == "wait" else zt != z)
            def _():
                {"start": copy.start, "wait": copy.wait_recv, "end": copy.wait_send}[action]()

            if action == "start":

                @pl.when(zt == z)
                def _():
                    dst[zlo] = src[block]

    gate_up = (ws, wr, ws_s, ws_r)
    down_w = (us, ur, us_s, us_r)

    for c in loads[6:]:
        c.wait()
    qf = jnp.concatenate(
        [
            q_v[2 * half + tt, :, pl.ds(pl.multiple_of(k * 256 + 128 * gg, 128), 128)].astype(F32)
            for tt in range(2) for gg in range(2)
        ],
        axis=0,
    ).astype(BF16)
    nk = nk_v[...].astype(F32).reshape(32, 128).astype(BF16)
    nv = nv_v[...].astype(F32).reshape(32, 128).astype(BF16)
    fs = lax.dot_general(qf, nk, NT, preferred_element_type=F32) * SCALE
    frow = lax.broadcasted_iota(jnp.int32, (32, 32), 0)
    fcl = lax.broadcasted_iota(jnp.int32, (32, 32), 1)
    fmask = ((fcl & 7) == (frow & 7)) & (lax.shift_right_logical(fcl, 3) <= lax.shift_right_logical(frow, 4) + 2 * half)
    fs = jnp.where(fmask, fs, NEG_FILL)
    ftop = jnp.max(fs, axis=1, keepdims=True)
    fw = jnp.where(fmask, jnp.exp(fs - ftop), 0.0).astype(BF16)
    ftot = jnp.sum(fw.astype(F32), axis=1, keepdims=True)
    facc = jnp.dot(fw, nv, preferred_element_type=F32)
    fstat = stats(ftop, ftot)

    def merge(parts):
        peak = functools.reduce(jnp.maximum, parts)
        fac = [jnp.exp(v - peak) for v in parts]
        total = sum(pltpu.roll(f, 48, 1) * v for f, v in zip(fac, parts))
        return peak, fac, total

    pl.semaphore_wait(near1, 2)
    tell(near2)
    ra[0] = pa[k, half]
    for c in ca:
        c.wait_recv()
    peak, fac, total = merge([join3(ra[d, 4].astype(F32)) for d in range(16)])
    for i in range(4):
        pb[i] = sum(fac[d][:, i:i + 1] * ra[d, i].astype(F32) for d in range(16)).astype(BF16)
    pb[4] = split3(jnp.where(lane < 4, peak, jnp.where((lane >= 48) & (lane < 52), total, 0.0)))

    cb = send([remote(pb, rb.at[zh], b_s.at[d], b_r.at[d], peer) for d, peer in z_peers])
    pl.semaphore_wait(near2, 2)
    weights(*gate_up, "start")
    rb[zh] = pb[...]
    for c in cb:
        c.wait_recv()
    _, fac, total = merge([join3(rb[d, 4].astype(F32)) for d in range(4)] + [fstat])
    inverse = pltpu.roll(total, 80, 1)
    for i in range(4):
        acc = sum(fac[d][:, i:i + 1] * rb[d, i].astype(F32) for d in range(4))
        acc = acc + fac[4][:, i:i + 1] * facc[8 * i:8 * i + 8]
        attn = (acc / inverse[:, i:i + 1]).astype(BF16).astype(F32)
        tt, gg = i // 2, i % 2
        x_v[q, 2 * half + tt, :, 128 * gg:128 * gg + 128] = (
            res_v[tt, :, 128 * gg:128 * gg + 128].astype(F32) + attn
        ).astype(BF16)

    mine = x_v.at[q, pl.ds(2 * half, 2)]
    cd = send([remote(mine, mine, d_s.at[d], d_r.at[d], peer) for d, _, _, peer in c_peers])
    weights(*down_w, "start")
    for c in cd:
        c.wait_recv()
    weights(*gate_up, "wait")

    xf = x_v[...].astype(F32).reshape(256, 256)
    square = jnp.sum(xf * xf, axis=1, keepdims=True)
    xg = (xf * gain_v[fcol].astype(F32).reshape(1, 256)).astype(BF16)
    gu = jnp.dot(xg, wr[...].reshape(256, 256), preferred_element_type=F32)
    hi = square.astype(BF16).astype(F32)
    lane2 = lax.broadcasted_iota(jnp.int32, (256, 256), 1)
    gu = jnp.where(lane2 == 96, hi, jnp.where(lane2 == 97, square - hi, gu))
    pp[...] = gu.astype(BF16).reshape(8, 32, 256)
    ce = send([remote(pp.at[kt], rp.at[d], e_s.at[d], e_r.at[d], peer) for d, kt, peer in k_peers])
    rp[0] = pp[k]
    for c in ce:
        c.wait_recv()
    gu = jnp.sum(rp[...].astype(F32), axis=0)
    lane32 = lax.broadcasted_iota(jnp.int32, (32, 128), 1)
    gate, up = gu[:, :128], gu[:, 128:]
    square = jnp.sum(jnp.where((lane32 == 96) | (lane32 == 97), gate, 0.0), axis=1, keepdims=True)
    norm = lax.rsqrt(square * (1.0 / 2048) + EPSILON)
    gate = gate * norm
    up = up * norm
    hidden = gate / (1.0 + jnp.exp(-gate)) * up
    hh[k] = jnp.where(lane32 < 96, hidden, 0.0).astype(BF16)
    cf = send([remote(hh.at[k], hh.at[k], f_s.at[d], f_r.at[d], peer) for d, _, peer in k_peers])
    for c in cf:
        c.wait_recv()

    weights(*down_w, "wait")
    down = lax.dot_general(
        hh[...].reshape(256, 128), ur[...].reshape(256, 128), NT, preferred_element_type=F32
    )
    dd[...] = down.astype(BF16).reshape(8, 2, 16, 256)
    cg = send([remote(dd.at[qt, ht], rd.at[d], g_s.at[d], g_r.at[d], peer) for d, qt, ht, peer in c_peers])
    rd[0] = dd[q, half]
    for c in cg:
        c.wait_recv()
    ee[...] = jnp.sum(rd[...].astype(F32), axis=0).astype(BF16)
    ch = send([remote(ee, re.at[zh], h_s.at[d], h_r.at[d], peer) for d, peer in z_peers])
    re[zh] = ee[...]
    for c in ch:
        c.wait_recv()
    final = mine[...].astype(F32) + jnp.sum(re[...].astype(F32), axis=0).reshape(2, 8, 256)
    piece = out.at[pl.ds(2 * half, 2), :, fcol]
    piece[...] = final.astype(BF16)

    ci = send([remote(piece, piece, c_s.at[d], c_r.at[d], peer) for d, _, _, peer in a_peers])
    for c in ci:
        c.wait_recv()

    for c in sent:
        c.wait_send()
    weights(*gate_up, "end")
    weights(*down_w, "end")


def step(q, nk, nv, kc, vc, cache_len, resid, gain, w_gate, w_up, w_down):
    hbm = pl.BlockSpec(memory_space=pl.ANY)
    dma = lambda n: pltpu.SemaphoreType.DMA((n,))
    vm = pltpu.VMEM
    sems = []
    for n in (8, 8, 16, 4, 16, 16, 8, 8, 16, 4):
        sems += [dma(n), dma(n)]
    return pl.pallas_call(
        kernel,
        out_shape=jax.ShapeDtypeStruct((4, 8, 2048), BF16),
        in_specs=[hbm] * 5 + [pl.BlockSpec(memory_space=pltpu.SMEM)] + [hbm] * 5,
        out_specs=pl.BlockSpec(memory_space=pltpu.VMEM),
        scratch_shapes=[
            vm((4, 8, 2048), BF16), vm((4, 8, 128), BF16), vm((4, 8, 128), BF16),
            vm((8, 32, 1024), BF16), vm((8, 32, 1024), BF16), vm((2, 8, 256), BF16), vm((2048,), BF16),
            vm((32, 768), BF16), vm((32, 768), BF16), vm((32, 768), BF16),
            vm((8, 32, 256), BF16), vm((8, 32, 256), BF16), vm((8, 32, 128), BF16), vm((8, 32, 128), BF16),
            vm((8, 2, 5, 8, 128), BF16), vm((16, 5, 8, 128), BF16),
            vm((5, 8, 128), BF16), vm((4, 5, 8, 128), BF16),
            vm((8, 4, 8, 256), BF16),
            vm((8, 32, 256), BF16), vm((8, 32, 256), BF16),
            vm((8, 32, 128), BF16),
            vm((8, 2, 16, 256), BF16), vm((16, 16, 256), BF16),
            vm((16, 256), BF16), vm((4, 16, 256), BF16),
            dma(10), pltpu.SemaphoreType.REGULAR, pltpu.SemaphoreType.REGULAR,
        ] + sems,
        compiler_params=pltpu.CompilerParams(
            collective_id=0, has_side_effects=True, vmem_limit_bytes=16 * 1024 * 1024
        ),
    )(*[pltpu.with_memory_space_constraint(a, pltpu.HBM) for a in (q, nk, nv, kc, vc, cache_len, resid, gain, w_gate, w_up, w_down.T)])


def solution(mesh):
    placed = (
        P(None, "req", None),
        P(None, "req", None),
        P(None, "req", None),
        P("req", "seq", None),
        P("req", "seq", None),
        P("req"),
        P(None, "req", None),
        P(),
        P("seq", "req"),
        P("seq", "req"),
        P("req", "seq"),
    )
    return jax.shard_map(step, mesh=mesh, in_specs=placed, out_specs=P(None, "req", None), check_vma=False)
```

```python
import functools
import math

import jax
import jax.numpy as jnp
from jax import lax
from jax.experimental import pallas as pl
from jax.experimental.pallas import tpu as pltpu
from jax.sharding import PartitionSpec as P

NEG_FILL = -1e30
EPSILON = 1e-06
F32 = jnp.float32
BF16 = jnp.bfloat16
NT = (((1,), (1,)), ((), ()))
SCALE = 1.0 / math.sqrt(128)


def split3(x):
    hi = x.astype(BF16).astype(F32)
    rest = x - hi
    mid = rest.astype(BF16).astype(F32)
    low = (rest - mid).astype(BF16).astype(F32)
    return (hi + pltpu.roll(mid, 16, 1) + pltpu.roll(low, 32, 1)).astype(BF16)


def join3(x):
    return x + pltpu.roll(x, 112, 1) + pltpu.roll(x, 96, 1)


def kernel(
    q_h, nk_h, nv_h, k_h, v_h, len_s, resid_h, gain_h, wg_h, wu_h, wd_h,
    out,
    q_v, nk_v, nv_v, k_v, v_v, res_v, gain_v, wg_v, wu_v, wd_v,
    ws, wr, us, ur, pa, ra, pb, rb, x_v, pp, rp, hh, dd, rd, ee, re,
    lsem, near1, near2,
    ws_s, ws_r, us_s, us_r, a_s, a_r, b_s, b_r, c_s, c_r, d_s, d_r, e_s, e_r, f_s, f_r, g_s, g_r, h_s, h_r,
):
    s = lax.axis_index("seq")
    q = lax.axis_index("req")
    y = lax.div(s, 16)
    z = lax.rem(s, 16)
    kb = lax.rem(z, 2)
    k = y * 2 + kb
    zpair = z + 1 - 2 * kb
    zh = lax.div(z, 4)
    zl = lax.rem(z, 4)
    half = lax.div(zl, 2)
    zhi = lax.div(z, 8)
    zlo = lax.rem(z, 8)

    def at(yy, zz):
        return yy * 16 + zz

    a_peers = []
    for dy in range(4):
        for dz in range(4):
            if dy or dz:
                yt, zt = lax.rem(y + dy, 4), lax.rem(zl + dz, 4)
                kt, ht = yt * 2 + lax.rem(zt, 2), lax.div(zt, 2)
                a_peers.append((4 * dy + dz, kt, ht, (at(yt, 4 * zh + zt), q)))
    a_peers.sort(key=lambda p: -(min(p[0] // 4, 4 - p[0] // 4) * 2 + min(p[0] % 4, 2)))
    z_peers = [(d, (at(y, lax.rem(z + 4 * d, 16)), q)) for d in (2, 1, 3)]
    c_peers = []
    for dq in range(8):
        for dh in range(2):
            if dq or dh:
                qt = lax.rem(q + dq, 8)
                ht = 1 - half if dh else half
                c_peers.append((2 * dq + dh, qt, ht, (at(y, 4 * zh + 2 * ht + kb), qt)))
    c_peers.sort(key=lambda p: -(min(p[0] // 4, 4 - p[0] // 4) + 2 * (p[0] % 2)))
    k_peers = []
    for dy in range(4):
        for dk in range(2):
            if dy or dk:
                yt = lax.rem(y + dy, 4)
                kt = yt * 2 + (1 - kb if dk else kb)
                k_peers.append((2 * dy + dk, kt, (at(yt, zpair if dk else z), q)))
    k_peers.sort(key=lambda p: -(min(p[0] // 2, 4 - p[0] // 2) + p[0] % 2))
    steps_z = [p[-1] for p in z_peers if p[0] != 2]

    kcol = pl.ds(pl.multiple_of(k * 128, 128), 128)
    fcol = pl.ds(pl.multiple_of(k * 256, 256), 256)
    loads = [
        (wg_h, wg_v), (wu_h, wu_v), (wd_h, wd_v), (q_h, q_v), (k_h, k_v), (v_h, v_v),
        (nk_h.at[:, :, kcol], nk_v), (nv_h.at[:, :, kcol], nv_v),
        (resid_h.at[pl.ds(2 * half, 2), :, fcol], res_v), (gain_h, gain_v),
    ]
    loads = [pltpu.make_async_copy(a, b, lsem.at[i]) for i, (a, b) in enumerate(loads)]
    for c in loads:
        c.start()

    barrier = pltpu.get_barrier_semaphore()
    same = [p for p in c_peers if p[0] == 1][0]
    greeted = [p[-1] for p in a_peers + c_peers if p is not same] + steps_z
    for peer in greeted:
        pl.semaphore_signal(barrier, inc=1, device_id=peer, device_id_type=pl.DeviceIdType.MESH)

    def remote(src, dst, ssem, rsem, peer):
        return pltpu.make_async_remote_copy(
            src_ref=src, dst_ref=dst, send_sem=ssem, recv_sem=rsem,
            device_id=peer, device_id_type=pl.DeviceIdType.MESH,
        )

    def tell(sem):
        for peer in steps_z:
            pl.semaphore_signal(sem, inc=1, device_id=peer, device_id_type=pl.DeviceIdType.MESH)

    sent = []

    def send(copies):
        for c in copies:
            c.start()
        sent.extend(copies)
        return copies

    for c in loads[3:6]:
        c.wait()
    row = lax.broadcasted_iota(jnp.int32, (64, 256), 0) & 7
    col = lax.broadcasted_iota(jnp.int32, (64, 256), 1)
    limit = jnp.zeros((64, 256), jnp.int32)
    for r in range(8):
        limit = jnp.where(row == r, len_s[r], limit)
    mask = (lax.shift_right_logical(col, 5) == row) & ((col & 31) + s * 32 < limit)
    lane = lax.broadcasted_iota(jnp.int32, (8, 128), 1)

    def stats(top, tot):
        tile = jnp.zeros((8, 128), F32)
        for i in range(4):
            tile = jnp.where(lane == i, top[8 * i:8 * i + 8], tile)
            tile = jnp.where(lane == 48 + i, tot[8 * i:8 * i + 8], tile)
        return tile

    for kv in range(8):
        qk = jnp.concatenate(
            [
                q_v[tt, :, 128 * (2 * kv + gg):128 * (2 * kv + gg) + 128].astype(F32)
                for tt in range(4) for gg in range(2)
            ],
            axis=0,
        ).astype(BF16)
        keys = k_v[:, :, 128 * kv:128 * kv + 128].reshape(256, 128)
        vals = v_v[:, :, 128 * kv:128 * kv + 128].reshape(256, 128)
        sc = lax.dot_general(qk, keys, NT, preferred_element_type=F32) * SCALE
        sc = jnp.where(mask, sc, NEG_FILL)
        top = jnp.max(sc, axis=1, keepdims=True)
        w = jnp.where(mask, jnp.exp(sc - top), 0.0).astype(BF16)
        tot = jnp.sum(w.astype(F32), axis=1, keepdims=True)
        acc = jnp.dot(w, vals, preferred_element_type=F32).astype(BF16)
        for h in range(2):
            pa[kv, h, 0:4] = acc[32 * h:32 * h + 32].reshape(4, 8, 128)
            pa[kv, h, 4] = split3(stats(top[32 * h:32 * h + 32], tot[32 * h:32 * h + 32]))

    pl.semaphore_wait(barrier, len(greeted))

    ca = send([remote(pa.at[kt, ht], ra.at[d], a_s.at[d], a_r.at[d], peer) for d, kt, ht, peer in a_peers])

    tell(near1)

    for c in loads[:3]:
        c.wait()
    whole = [wg_v[...].astype(F32), wu_v[...].astype(F32), wd_v[...].astype(F32)]
    keep = lax.broadcasted_iota(jnp.int32, (32, 128), 1) < 96
    for j in range(8):
        base, off = (96 * j) // 128 * 128, (96 * j) % 128
        for i, w in enumerate(whole):
            if off + 96 <= 128:
                piece = w[:, base:base + 128]
                if off:
                    piece = pltpu.roll(piece, 128 - off, 1)
            else:
                piece = pltpu.roll(w[:, base:base + 256], 256 - off, 1)[:, :128]
            part = jnp.where(keep, piece, 0.0).astype(BF16)
            if i < 2:
                ws[j, :, 128 * i:128 * i + 128] = part
            else:
                us[j] = part

    def weights(src, dst, ssem, rsem, action):
        for j in range(8):
            block = lax.rem(lax.div(z, 2) + (4, 3, 5, 2, 6, 1, 7, 0)[j], 8)
            zt = 2 * block + zhi
            copy = remote(src.at[block], dst.at[zlo], ssem.at[j], rsem.at[zlo], (at(y, zt), q))
            if action == "wait":
                copy = remote(src.at[j], dst.at[j], ssem.at[j], rsem.at[j], (s, q))

            @pl.when(8 * kb + j != z if action == "wait" else zt != z)
            def _():
                {"start": copy.start, "wait": copy.wait_recv, "end": copy.wait_send}[action]()

            if action == "start":

                @pl.when(zt == z)
                def _():
                    dst[zlo] = src[block]

    gate_up = (ws, wr, ws_s, ws_r)
    down_w = (us, ur, us_s, us_r)

    for c in loads[6:]:
        c.wait()
    qf = jnp.concatenate(
        [
            q_v[2 * half + tt, :, pl.ds(pl.multiple_of(k * 256 + 128 * gg, 128), 128)].astype(F32)
            for tt in range(2) for gg in range(2)
        ],
        axis=0,
    ).astype(BF16)
    nk = nk_v[...].astype(F32).reshape(32, 128).astype(BF16)
    nv = nv_v[...].astype(F32).reshape(32, 128).astype(BF16)
    fs = lax.dot_general(qf, nk, NT, preferred_element_type=F32) * SCALE
    frow = lax.broadcasted_iota(jnp.int32, (32, 32), 0)
    fcl = lax.broadcasted_iota(jnp.int32, (32, 32), 1)
    fmask = ((fcl & 7) == (frow & 7)) & (lax.shift_right_logical(fcl, 3) <= lax.shift_right_logical(frow, 4) + 2 * half)
    fs = jnp.where(fmask, fs, NEG_FILL)
    ftop = jnp.max(fs, axis=1, keepdims=True)
    fw = jnp.where(fmask, jnp.exp(fs - ftop), 0.0).astype(BF16)
    ftot = jnp.sum(fw.astype(F32), axis=1, keepdims=True)
    facc = jnp.dot(fw, nv, preferred_element_type=F32)
    fstat = stats(ftop, ftot)

    def merge(parts):
        peak = functools.reduce(jnp.maximum, parts)
        fac = [jnp.exp(v - peak) for v in parts]
        total = sum(pltpu.roll(f, 48, 1) * v for f, v in zip(fac, parts))
        return peak, fac, total

    pl.semaphore_wait(near1, 2)
    tell(near2)
    ra[0] = pa[k, half]
    for c in ca:
        c.wait_recv()
    peak, fac, total = merge([join3(ra[d, 4].astype(F32)) for d in range(16)])
    for i in range(4):
        pb[i] = sum(fac[d][:, i:i + 1] * ra[d, i].astype(F32) for d in range(16)).astype(BF16)
    pb[4] = split3(jnp.where(lane < 4, peak, jnp.where((lane >= 48) & (lane < 52), total, 0.0)))

    cb = send([remote(pb, rb.at[zh], b_s.at[d], b_r.at[d], peer) for d, peer in z_peers])
    pl.semaphore_wait(near2, 2)
    weights(*gate_up, "start")
    rb[zh] = pb[...]
    for c in cb:
        c.wait_recv()
    _, fac, total = merge([join3(rb[d, 4].astype(F32)) for d in range(4)] + [fstat])
    inverse = pltpu.roll(total, 80, 1)
    for i in range(4):
        acc = sum(fac[d][:, i:i + 1] * rb[d, i].astype(F32) for d in range(4))
        acc = acc + fac[4][:, i:i + 1] * facc[8 * i:8 * i + 8]
        attn = (acc / inverse[:, i:i + 1]).astype(BF16).astype(F32)
        tt, gg = i // 2, i % 2
        x_v[q, 2 * half + tt, :, 128 * gg:128 * gg + 128] = (
            res_v[tt, :, 128 * gg:128 * gg + 128].astype(F32) + attn
        ).astype(BF16)

    mine = x_v.at[q, pl.ds(2 * half, 2)]
    cd = send([remote(mine, mine, d_s.at[d], d_r.at[d], peer) for d, _, _, peer in c_peers])
    weights(*down_w, "start")
    for c in cd:
        c.wait_recv()
    weights(*gate_up, "wait")

    xf = x_v[...].astype(F32).reshape(256, 256)
    square = jnp.sum(xf * xf, axis=1, keepdims=True)
    xg = (xf * gain_v[fcol].astype(F32).reshape(1, 256)).astype(BF16)
    gu = jnp.dot(xg, wr[...].reshape(256, 256), preferred_element_type=F32)
    hi = square.astype(BF16).astype(F32)
    lane2 = lax.broadcasted_iota(jnp.int32, (256, 256), 1)
    gu = jnp.where(lane2 == 96, hi, jnp.where(lane2 == 97, square - hi, gu))
    pp[...] = gu.astype(BF16).reshape(8, 32, 256)
    ce = send([remote(pp.at[kt], rp.at[d], e_s.at[d], e_r.at[d], peer) for d, kt, peer in k_peers])
    rp[0] = pp[k]
    for c in ce:
        c.wait_recv()
    gu = jnp.sum(rp[...].astype(F32), axis=0)
    lane32 = lax.broadcasted_iota(jnp.int32, (32, 128), 1)
    gate, up = gu[:, :128], gu[:, 128:]
    square = jnp.sum(jnp.where((lane32 == 96) | (lane32 == 97), gate, 0.0), axis=1, keepdims=True)
    norm = lax.rsqrt(square * (1.0 / 2048) + EPSILON)
    gate = gate * norm
    up = up * norm
    hidden = gate / (1.0 + jnp.exp(-gate)) * up
    hh[k] = jnp.where(lane32 < 96, hidden, 0.0).astype(BF16)
    cf = send([remote(hh.at[k], hh.at[k], f_s.at[d], f_r.at[d], peer) for d, _, peer in k_peers])
    for c in cf:
        c.wait_recv()

    weights(*down_w, "wait")
    down = lax.dot_general(
        hh[...].reshape(256, 128), ur[...].reshape(256, 128), NT, preferred_element_type=F32
    )
    dd[...] = down.astype(BF16).reshape(8, 2, 16, 256)
    cg = send([remote(dd.at[qt, ht], rd.at[d], g_s.at[d], g_r.at[d], peer) for d, qt, ht, peer in c_peers])
    rd[0] = dd[q, half]
    for c in cg:
        c.wait_recv()
    ee[...] = jnp.sum(rd[...].astype(F32), axis=0).astype(BF16)
    older = list(sent)
    sent.clear()
    ch = send([remote(ee, re.at[zh], h_s.at[d], h_r.at[d], peer) for d, peer in z_peers])
    re[zh] = ee[...]
    for c in older:
        c.wait_send()
    weights(*gate_up, "end")
    weights(*down_w, "end")
    for c in ch:
        c.wait_recv()
    final = mine[...].astype(F32) + jnp.sum(re[...].astype(F32), axis=0).reshape(2, 8, 256)
    piece = out.at[pl.ds(2 * half, 2), :, fcol]
    piece[...] = final.astype(BF16)

    ci = send([remote(piece, piece, c_s.at[d], c_r.at[d], peer) for d, _, _, peer in a_peers])
    for c in sent:
        c.wait_send()
    for c in ci:
        c.wait_recv()


def step(q, nk, nv, kc, vc, cache_len, resid, gain, w_gate, w_up, w_down):
    hbm = pl.BlockSpec(memory_space=pl.ANY)
    dma = lambda n: pltpu.SemaphoreType.DMA((n,))
    vm = pltpu.VMEM
    sems = []
    for n in (8, 8, 16, 4, 16, 16, 8, 8, 16, 4):
        sems += [dma(n), dma(n)]
    return pl.pallas_call(
        kernel,
        out_shape=jax.ShapeDtypeStruct((4, 8, 2048), BF16),
        in_specs=[hbm] * 5 + [pl.BlockSpec(memory_space=pltpu.SMEM)] + [hbm] * 5,
        out_specs=pl.BlockSpec(memory_space=pltpu.VMEM),
        scratch_shapes=[
            vm((4, 8, 2048), BF16), vm((4, 8, 128), BF16), vm((4, 8, 128), BF16),
            vm((8, 32, 1024), BF16), vm((8, 32, 1024), BF16), vm((2, 8, 256), BF16), vm((2048,), BF16),
            vm((32, 768), BF16), vm((32, 768), BF16), vm((32, 768), BF16),
            vm((8, 32, 256), BF16), vm((8, 32, 256), BF16), vm((8, 32, 128), BF16), vm((8, 32, 128), BF16),
            vm((8, 2, 5, 8, 128), BF16), vm((16, 5, 8, 128), BF16),
            vm((5, 8, 128), BF16), vm((4, 5, 8, 128), BF16),
            vm((8, 4, 8, 256), BF16),
            vm((8, 32, 256), BF16), vm((8, 32, 256), BF16),
            vm((8, 32, 128), BF16),
            vm((8, 2, 16, 256), BF16), vm((16, 16, 256), BF16),
            vm((16, 256), BF16), vm((4, 16, 256), BF16),
            dma(10), pltpu.SemaphoreType.REGULAR, pltpu.SemaphoreType.REGULAR,
        ] + sems,
        compiler_params=pltpu.CompilerParams(
            collective_id=0, has_side_effects=True, vmem_limit_bytes=16 * 1024 * 1024
        ),
    )(*[pltpu.with_memory_space_constraint(a, pltpu.HBM) for a in (q, nk, nv, kc, vc, cache_len, resid, gain, w_gate, w_up, w_down.T)])


def solution(mesh):
    placed = (
        P(None, "req", None),
        P(None, "req", None),
        P(None, "req", None),
        P("req", "seq", None),
        P("req", "seq", None),
        P("req"),
        P(None, "req", None),
        P(),
        P("seq", "req"),
        P("seq", "req"),
        P("req", "seq"),
    )
    return jax.shard_map(step, mesh=mesh, in_specs=placed, out_specs=P(None, "req", None), check_vma=False)
```
